256 devices in a mesh: context: 32 (over x, z), mirror: 2 (over core), tensor: 4 (over y).
Axes of the slice: x: 4, y: 4, z: 8, core: 2. Of those that a mesh axis runs over, the one named last changes fastest.
Arguments:
- hyena_q: bfloat16 [8192, 8192], P(('context', 'mirror'), 'tensor'), may hold values from -57 to 57
- hyena_k: bfloat16 [8192, 8192], P(('context', 'mirror'), 'tensor'), may hold values from -6 to 6
- hyena_v: bfloat16 [8192, 8192], P(('context', 'mirror'), 'tensor'), may hold values from -6 to 6
- filters: bfloat16 [512, 128], P('tensor'), may hold values from -0.5 to 0.5
- norm_gain: float32 [8192], P('tensor'), may hold values from 0.1 to 1.9
- attn_q: bfloat16 [8192, 8192], P(('context', 'mirror'), 'tensor'), may hold values from -35 to 35
- attn_k: bfloat16 [8192, 8192], P(('context', 'mirror'), 'tensor'), may hold values from -5 to 5
- out_grad: bfloat16 [8192, 8192], P(('context', 'mirror'), 'tensor'), may hold values from -20 to 20
- doc_lengths: int32 [4], replicated, may hold values from 1 to 4096, 8192 in all
Outputs:
- attn_out: bfloat16 [8192, 8192], P(('context', 'mirror'), 'tensor')
- grad_attn_q: bfloat16 [8192, 8192], P(('context', 'mirror'), 'tensor')
- grad_attn_k: bfloat16 [8192, 8192], P(('context', 'mirror'), 'tensor')
- grad_hyena_q: bfloat16 [8192, 8192], P(('context', 'mirror'), 'tensor')
- grad_hyena_k: bfloat16 [8192, 8192], P(('context', 'mirror'), 'tensor')
- grad_hyena_v: bfloat16 [8192, 8192], P(('context', 'mirror'), 'tensor')
- grad_filters: float32 [512, 128], P('tensor')
The draws below stay inside these ranges and needn't reach their ends.
All inputs are finite; a program needn't handle non-finite values.
Results may differ from the reference program's by a relative error of at most 0.0064.
Values may be sent and summed in bfloat16 or wider, within the bound.
No kernel may reach another device: no remote copies, remote signals or barrier semaphores. Data moves between devices by JAX's collectives and lax.ppermute only.
A program may use at most 128 MiB of HBM per device.

```python
import math
import jax
import jax.numpy as jnp
import numpy as np
from jax import lax

HEADS = 64
HEAD = 128
TAPS = 128
D = 8192
GROUP = 16
FILTERS = 512
T_DEV = 128
REACH = 2
DOCS = 4
SEQ = 8192
DOC_MOST = 4096


def draw_hyena_q(key, part):
    key_base, key_cols, key_rows = jax.random.split(key, 3)
    col_frac = jnp.arange(D, dtype=jnp.float32) / max(D - 1, 1)
    col_scale = 3.0 ** col_frac * jnp.exp(jax.random.uniform(key_cols, (D,), minval=-0.4, maxval=0.4))
    row_scale = 10.0 ** jax.random.uniform(key_rows, (SEQ,))
    base_draw = jnp.clip(jax.random.normal(key_base, (SEQ, D)), -5.0, 5.0)
    return (base_draw * col_scale[None, :] * row_scale[:, None] / 4.0).astype(jnp.bfloat16)


def drawn_pair(key):
    pair_key = jax.random.fold_in(key, 11)
    key_keys, key_queries = jax.random.split(pair_key)
    key_rows = jnp.clip(jax.random.normal(key_keys, (SEQ, D)), -5.0, 5.0)
    query_rows = jnp.clip(jax.random.normal(key_queries, (SEQ, D)), -5.0, 5.0)
    return (query_rows, key_rows)


def draw_attn_q(key, part):
    return drawn_pair(key)[0].astype(jnp.bfloat16)


def draw_attn_k(key, part):
    return drawn_pair(key)[1].astype(jnp.bfloat16)


def draw_out_grad(key, part):
    key_base, key_rows = jax.random.split(key, 2)
    position_frac = jnp.arange(SEQ, dtype=jnp.float32) / max(SEQ - 1, 1)
    row_scale = 3.0 ** position_frac * 10.0 ** jax.random.uniform(key_rows, (SEQ,)) / 8.0
    base_draw = jnp.clip(jax.random.normal(key_base, (SEQ, D)), -5.0, 5.0)
    return (base_draw * row_scale[:, None]).astype(jnp.bfloat16)


def block_levels(key, extent, cuts, low, largest):
    def one(axis_at, shards_of):
        draws = jax.random.uniform(jax.random.fold_in(jax.random.fold_in(key, 6), axis_at), (shards_of,), jnp.float32, low / len(cuts), largest / len(cuts))
        return jnp.repeat(jnp.exp(draws), extent[axis_at] // shards_of).reshape((-1,) + (1,) * (len(extent) - axis_at - 1))

    level = one(*cuts[0])
    for cut in cuts[1:]:
        level = level * one(*cut)
    return level


def length_profile(amount, total, most, slope):
    portions = [(1 << 20) // math.isqrt(standing ** slope) + 1 for standing in range(2, amount + 1)]
    surplus, holding = total - most - (amount - 1), [1] * (amount - 1)
    while surplus > 0:
        movable = [i for i in range(amount - 1) if holding[i] < most]
        pool, left = sum([portions[i] for i in movable]), surplus
        for i in movable:
            addition = min(most - holding[i], max(1, left * portions[i] // pool), surplus)
            holding[i] = holding[i] + addition
            surplus = surplus - addition
    return np.array([most] + holding)


def uneven(stream_key, count, total, reach, skew):
    if count == 2:
        one = jax.random.randint(stream_key, (), max(1, total - reach), min(reach, total - 1) + 1)
        return jnp.stack([one, total - one])
    tallies = jnp.asarray(length_profile(count, total, reach, skew), jnp.int32)
    twos = (count - 1) // 2
    donor, taker = tallies[1:1 + 2 * twos:2], tallies[2:2 + 2 * twos:2]
    room = jnp.minimum(donor - 1, reach - taker)
    passed = jax.random.randint(jax.random.fold_in(stream_key, 1), (twos,), 0, 1 << 20) % (room + 1)
    tallies = tallies.at[1:1 + 2 * twos:2].set(donor - passed).at[2:2 + 2 * twos:2].set(taker + passed)
    return tallies[jax.random.permutation(jax.random.fold_in(stream_key, 2), count)]


def scatter_about(rng, dims, width, most, cuts=(), kind=jnp.bfloat16):
    values = jax.random.normal(rng, dims, jnp.float32) * width
    if len(cuts) > 0:
        values = block_levels(rng, dims, cuts, -0.22, 0.18) * values
    return jnp.clip(values, min=-most, max=most).astype(kind)


def setup_inputs(seed: int = 0) -> dict:
    arg_keys = jax.random.split(jax.random.key(seed), 10)
    hyena_q = draw_hyena_q(jax.random.fold_in(arg_keys[9], 71), 0)
    hyena_k = scatter_about(arg_keys[1], (SEQ, D), 1.0, 6.0, ((0, 64), (1, 4)))
    hyena_v = scatter_about(arg_keys[2], (SEQ, D), 1.0, 6.0, ((0, 64), (1, 4)))
    filters = scatter_about(arg_keys[3], (FILTERS, TAPS), TAPS ** -0.5, 0.5, ((0, 4),))
    norm_gain = jnp.clip(1.0 + 0.18 * jax.random.normal(arg_keys[4], (D,), jnp.float32), 0.1, 1.9)
    attn_q = draw_attn_q(jax.random.fold_in(arg_keys[9], 71), 0)
    attn_k = draw_attn_k(jax.random.fold_in(arg_keys[9], 71), 0)
    out_grad = draw_out_grad(jax.random.fold_in(arg_keys[9], 71), 0)
    doc_lengths = uneven(arg_keys[8], DOCS, SEQ, DOC_MOST, 2).astype(jnp.int32)
    return {"hyena_q": hyena_q, "hyena_k": hyena_k, "hyena_v": hyena_v, "filters": filters, "norm_gain": norm_gain, "attn_q": attn_q, "attn_k": attn_k, "out_grad": out_grad, "doc_lengths": doc_lengths}


def doc_index(doc_lengths, positions):
    doc_ends = jnp.cumsum(doc_lengths, dtype=jnp.int32)
    return lax.optimization_barrier(jnp.sum((positions[:, None] >= doc_ends[None, :]).astype(jnp.int32), axis=1, dtype=jnp.int32))

def forward_conv(wide_rows, filt_rows, doc_ids):
    width_rows = wide_rows.shape[0]
    padded = jnp.concatenate([jnp.zeros((width_rows, TAPS - 1), jnp.float32), wide_rows], axis=1)
    doc_pad = jnp.concatenate([jnp.full((TAPS - 1,), -1, jnp.int32), doc_ids])

    def tap_step(running, tap_index):
        shifted = lax.dynamic_slice_in_dim(padded, TAPS - 1 - tap_index, SEQ, 1)
        same_doc = lax.dynamic_slice_in_dim(doc_pad, TAPS - 1 - tap_index, SEQ, 0) == doc_ids
        tap_weight = lax.dynamic_slice_in_dim(filt_rows, tap_index, 1, 1)
        return (running + tap_weight * jnp.where(same_doc[None, :], shifted, 0.0), None)
    running, _ = lax.scan(tap_step, jnp.zeros_like(wide_rows), jnp.arange(TAPS, dtype=jnp.int32))
    return running

def backward_conv(grad_rows, wide_rows, filt_rows, doc_ids):
    width_rows = grad_rows.shape[0]
    grad_ahead = jnp.concatenate([grad_rows, jnp.zeros((width_rows, TAPS - 1), jnp.float32)], axis=1)
    doc_ahead = jnp.concatenate([doc_ids, jnp.full((TAPS - 1,), -1, jnp.int32)])
    behind = jnp.concatenate([jnp.zeros((width_rows, TAPS - 1), jnp.float32), wide_rows], axis=1)
    doc_behind = jnp.concatenate([jnp.full((TAPS - 1,), -1, jnp.int32), doc_ids])

    def tap_step(running, tap_index):
        shifted = lax.dynamic_slice_in_dim(grad_ahead, tap_index, SEQ, 1)
        same_doc = lax.dynamic_slice_in_dim(doc_ahead, tap_index, SEQ, 0) == doc_ids
        tap_weight = lax.dynamic_slice_in_dim(filt_rows, tap_index, 1, 1)
        running = running + tap_weight * jnp.where(same_doc[None, :], shifted, 0.0)
        earlier = lax.dynamic_slice_in_dim(behind, TAPS - 1 - tap_index, SEQ, 1)
        same_past = lax.dynamic_slice_in_dim(doc_behind, TAPS - 1 - tap_index, SEQ, 0) == doc_ids
        tap_corr = lax.optimization_barrier(jnp.sum(grad_rows * jnp.where(same_past[None, :], earlier, 0.0), axis=1))
        return (running, tap_corr)
    running, tap_corr = lax.scan(tap_step, jnp.zeros_like(grad_rows), jnp.arange(TAPS, dtype=jnp.int32))
    return (running, tap_corr.T)

def head_pass(query_all, key_all, value_all, grad_all, doc_ids):
    window = (REACH + 1) * T_DEV
    front = REACH * T_DEV
    score_scale = HEAD ** (-0.5)
    key_pad = jnp.concatenate([jnp.zeros((front, HEAD), jnp.bfloat16), key_all], axis=0)
    value_pad = jnp.concatenate([jnp.zeros((front, HEAD), jnp.bfloat16), value_all], axis=0)
    doc_pad = jnp.concatenate([jnp.full((front,), -1, jnp.int32), doc_ids])

    def block_step(carry, block_index):
        key_acc, value_acc = carry
        row_start = (block_index * T_DEV).astype(jnp.int32)
        query_block = lax.dynamic_slice_in_dim(query_all, row_start, T_DEV, 0)
        grad_block = lax.dynamic_slice_in_dim(grad_all, row_start, T_DEV, 0)
        query_doc = lax.dynamic_slice_in_dim(doc_ids, row_start, T_DEV, 0)
        key_block = lax.dynamic_slice_in_dim(key_pad, row_start, window, 0)
        value_block = lax.dynamic_slice_in_dim(value_pad, row_start, window, 0)
        key_doc = lax.dynamic_slice_in_dim(doc_pad, row_start, window, 0)
        query_pos = row_start + jnp.arange(T_DEV, dtype=jnp.int32)
        key_pos = row_start - front + jnp.arange(window, dtype=jnp.int32)
        allowed = (key_pos[None, :] <= query_pos[:, None]) & (query_pos[:, None] - key_pos[None, :] <= front) & (key_doc[None, :] == query_doc[:, None])
        scores = jnp.dot(query_block, key_block.T, preferred_element_type=jnp.float32) * score_scale
        row_top = lax.optimization_barrier(jnp.max(jnp.where(allowed, scores, -1e+30), axis=1, keepdims=True))
        row_total = lax.optimization_barrier(jnp.sum(jnp.exp(jnp.where(allowed, scores - row_top, -1e+30)), axis=1, keepdims=True))
        row_lse = row_top + jnp.log(row_total)
        prob = jnp.where(allowed, jnp.exp(scores - row_lse), 0.0)
        prob_half = prob.astype(jnp.bfloat16)
        out_block = jnp.dot(prob_half, value_block, preferred_element_type=jnp.float32).astype(jnp.bfloat16)
        grad_prob = jnp.dot(grad_block, value_block.T, preferred_element_type=jnp.float32)
        row_delta = lax.optimization_barrier(jnp.sum(prob * grad_prob, axis=1, keepdims=True))
        grad_score = (prob * (grad_prob - row_delta) * score_scale).astype(jnp.bfloat16)
        grad_query = jnp.dot(grad_score, key_block, preferred_element_type=jnp.float32).astype(jnp.bfloat16)
        key_part = jnp.dot(grad_score.T, query_block, preferred_element_type=jnp.float32)
        value_part = jnp.dot(prob_half.T, grad_block, preferred_element_type=jnp.float32)
        key_acc = lax.dynamic_update_slice_in_dim(key_acc, lax.dynamic_slice_in_dim(key_acc, row_start, window, 0) + key_part, row_start, 0)
        value_acc = lax.dynamic_update_slice_in_dim(value_acc, lax.dynamic_slice_in_dim(value_acc, row_start, window, 0) + value_part, row_start, 0)
        return ((key_acc, value_acc), (out_block, grad_query))
    start_acc = jnp.zeros((front + SEQ, HEAD), jnp.float32)
    (key_acc, value_acc), (out_blocks, query_blocks) = lax.scan(block_step, (start_acc, start_acc), jnp.arange(SEQ // T_DEV, dtype=jnp.int32))
    return (out_blocks.reshape(SEQ, HEAD), query_blocks.reshape(SEQ, HEAD), key_acc[front:], value_acc[front:])

def reference(hyena_q, hyena_k, hyena_v, filters, norm_gain, attn_q, attn_k, out_grad, doc_lengths):
    doc_ids = doc_index(doc_lengths, jnp.arange(SEQ, dtype=jnp.int32))
    block_size = min(D, 1024)
    block_count = D // block_size

    def to_blocks(array):
        return array.astype(jnp.float32).T.reshape(block_count, block_size, SEQ)

    def from_blocks(array):
        return array.reshape(D, SEQ).T
    filt_rows = jnp.repeat(filters.astype(jnp.float32), GROUP, axis=0).reshape(block_count, block_size, TAPS)
    kv_product = (hyena_k.astype(jnp.float32) * hyena_v.astype(jnp.float32)).astype(jnp.bfloat16)

    def conv_block(pieces):
        return forward_conv(pieces[0], pieces[1], doc_ids)
    signal = from_blocks(lax.map(conv_block, (to_blocks(kv_product), filt_rows)))
    hyena_mix = hyena_q.astype(jnp.float32) * signal
    inv_rms = lax.rsqrt(lax.optimization_barrier(jnp.sum(hyena_mix * hyena_mix, axis=1)) / D + 1e-06)
    values = (hyena_mix * inv_rms[:, None] * norm_gain[None, :]).astype(jnp.bfloat16)

    def to_heads(array):
        return array.reshape(SEQ, HEADS, HEAD).transpose(1, 0, 2)

    def from_heads(array):
        return array.transpose(1, 0, 2).reshape(SEQ, D)

    def attend_head(pieces):
        return head_pass(pieces[0], pieces[1], pieces[2], pieces[3], doc_ids)
    out_heads, query_heads, key_heads, value_heads = lax.map(attend_head, (to_heads(attn_q), to_heads(attn_k), to_heads(values), to_heads(out_grad)))
    attn_out = from_heads(out_heads)
    grad_attn_q = from_heads(query_heads)
    grad_attn_k = from_heads(key_heads).astype(jnp.bfloat16)
    grad_values = from_heads(value_heads)
    inner_sum = lax.optimization_barrier(jnp.sum(norm_gain[None, :] * grad_values * hyena_mix, axis=1))
    grad_mix = inv_rms[:, None] * (norm_gain[None, :] * grad_values - hyena_mix * (inner_sum * inv_rms * inv_rms / D)[:, None])
    grad_hyena_q = (grad_mix * signal).astype(jnp.bfloat16)
    grad_signal = (grad_mix * hyena_q.astype(jnp.float32)).astype(jnp.bfloat16)

    def back_block(pieces):
        return backward_conv(pieces[0], pieces[1], pieces[2], doc_ids)
    grad_kv, tap_corr = lax.map(back_block, (to_blocks(grad_signal), to_blocks(kv_product), filt_rows))
    grad_kv = from_blocks(grad_kv)
    grad_hyena_k = (grad_kv * hyena_v.astype(jnp.float32)).astype(jnp.bfloat16)
    grad_hyena_v = (grad_kv * hyena_k.astype(jnp.float32)).astype(jnp.bfloat16)
    grad_filters = lax.optimization_barrier(jnp.sum(tap_corr.reshape(D // GROUP, GROUP, TAPS), axis=1))
    return (attn_out, grad_attn_q, grad_attn_k, grad_hyena_q, grad_hyena_k, grad_hyena_v, grad_filters)
```

```python
import functools

import jax
import jax.numpy as jnp
from jax import lax
from jax.experimental import pallas as pl
from jax.experimental.pallas import tpu as pltpu
from jax.sharding import PartitionSpec as P

HEAD = 128
D = 8192
T = 128
LANES = 128
GROUP = 16
F32 = jnp.float32
BF16 = jnp.bfloat16
SEQ_AXES = ("context", "mirror")

VMEM = pl.BlockSpec(memory_space=pltpu.VMEM)
SMEM = pl.BlockSpec(memory_space=pltpu.SMEM)


def shifted(block, distance):
    count = lax.axis_size(SEQ_AXES)
    route = [(i - distance, i) for i in range(count) if 0 <= i - distance < count]
    return lax.ppermute(block, SEQ_AXES, route)


def across(block, distance):
    count = lax.axis_size("tensor")
    return lax.ppermute(block, "tensor", [(i, (i + distance) % count) for i in range(count)])


def call(body, ins, outs, flops, scratch=(), exps=0):
    nbytes = sum(a.size * a.dtype.itemsize for a in ins)
    nbytes += sum(o.size * o.dtype.itemsize for o in outs)
    specs = [SMEM if a.dtype == jnp.int32 else VMEM for a in ins]
    return pl.pallas_call(
        body,
        out_shape=tuple(outs),
        in_specs=specs,
        out_specs=tuple(VMEM for _ in outs),
        scratch_shapes=list(scratch),
        cost_estimate=pl.CostEstimate(flops=flops, bytes_accessed=nbytes, transcendentals=exps),
    )(*ins)


def sds(*shape, dtype=F32):
    return jax.ShapeDtypeStruct(shape, dtype)


def doc_of(info, pos):
    doc = (pos >= info[0]).astype(jnp.int32)
    for i in range(1, 4):
        doc = doc + (pos >= info[i]).astype(jnp.int32)
    return doc


def conv_mask(info, first, sign=1):
    rows = info[4] + lax.broadcasted_iota(jnp.int32, (T, 2 * T), 0)
    cols = first + sign * lax.broadcasted_iota(jnp.int32, (T, 2 * T), 1)
    return doc_of(info, rows) == doc_of(info, cols)


def column(row):
    return jnp.transpose(jnp.broadcast_to(row, (T, LANES)))


def banded_matmul(table_ref, mask, window, tile):
    bands = []
    for g in range(LANES // GROUP):
        row = table_ref[pl.ds(tile * 8 + g, 1), :]
        band = pltpu.roll(jnp.broadcast_to(row, (T, 2 * T)), 0, 1, stride=1, stride_axis=0)
        bands.append(jnp.where(mask, band, 0.0).astype(BF16))
    stacked = jnp.concatenate(bands, axis=0)
    full = jnp.dot(stacked, window, preferred_element_type=F32)
    lane_group = lax.broadcasted_iota(jnp.int32, (T, LANES), 1) // GROUP
    out = full[:T]
    for g in range(1, LANES // GROUP):
        out = jnp.where(lane_group == g, full[g * T : (g + 1) * T], out)
    return out


def lanes_of(tile):
    return pl.ds(pl.multiple_of(tile * LANES, LANES), LANES)


def conv_body(info, left, kv, hyena_q, table, signal, square, flipped):
    span = 2 * T
    turned = lax.broadcasted_iota(jnp.int32, (span, span), 0) + lax.broadcasted_iota(
        jnp.int32, (span, span), 1
    )
    turn = jnp.where(turned == span - 1, 1.0, 0.0).astype(BF16)
    mask = conv_mask(info, info[4] - T)
    tiles = kv.shape[1] // LANES

    def step(tile, acc):
        at = lanes_of(tile)
        window = jnp.concatenate([left[:, at], kv[:, at]], axis=0)
        out = banded_matmul(table, mask, window, tile)
        signal[:, at] = out
        flipped[:, at] = jnp.dot(turn, window, preferred_element_type=F32).astype(BF16)
        mix = hyena_q[:, at].astype(F32) * out
        return acc + mix * mix

    acc = lax.fori_loop(0, tiles, step, jnp.zeros((T, LANES), F32))
    square[...] = jnp.broadcast_to(jnp.sum(jnp.transpose(acc), axis=0, keepdims=True), (8, LANES))


def inv_rms_row(squares):
    total = squares[0][0:1, :]
    for s in squares[1:]:
        total = total + s[0:1, :]
    return lax.rsqrt(total / D + 1e-06)


def values_body(signal, hyena_q, gain, s0, s1, s2, s3, values):
    inv = column(inv_rms_row((s0, s1, s2, s3)))

    def step(tile, _):
        at = lanes_of(tile)
        mix = hyena_q[:, at].astype(F32) * signal[:, at]
        values[:, at] = (mix * inv * gain[:, at]).astype(BF16)
        return 0

    lax.fori_loop(0, signal.shape[1] // LANES, step, 0)


def scores_body(info, q, k0, k1, k2, og, prob, own, part1, part2):
    span = 3 * T
    query_pos = info[4] + lax.broadcasted_iota(jnp.int32, (span, T), 1)
    key_pos = info[4] - 2 * T + lax.broadcasted_iota(jnp.int32, (span, T), 0)
    allowed = (
        (key_pos >= 0)
        & (key_pos <= query_pos)
        & (query_pos - key_pos <= 2 * T)
        & (doc_of(info, key_pos) == doc_of(info, query_pos))
    )
    scale = HEAD**-0.5

    def step(h, _):
        at = lanes_of(h)
        keys = jnp.concatenate([k2[:, at], k1[:, at], k0[:, at]], axis=0)
        s = lax.dot_general(keys, q[:, at], (((1,), (1,)), ((), ())), preferred_element_type=F32)
        s = jnp.where(allowed, s * scale, -1e30)
        top = jnp.max(s, axis=0, keepdims=True)
        e = jnp.exp(s - top)
        p = e * (1.0 / jnp.sum(e, axis=0, keepdims=True))
        prob[h] = p
        part = jnp.dot(p.astype(BF16), og[:, at], preferred_element_type=F32)
        part2[:, at] = part[:T].astype(BF16)
        part1[:, at] = part[T : 2 * T].astype(BF16)
        own[:, at] = part[2 * T :]
        return 0

    lax.fori_loop(0, q.shape[1] // HEAD, step, 0)


def inner_body(own, part1, part2, signal, hyena_q, gain, grad_values, inner):
    def step(tile, acc):
        at = lanes_of(tile)
        gv = own[:, at] + part1[:, at].astype(F32) + part2[:, at].astype(F32)
        gv = gv * gain[:, at]
        grad_values[:, at] = gv
        return acc + gv * (hyena_q[:, at].astype(F32) * signal[:, at])

    acc = lax.fori_loop(0, own.shape[1] // LANES, step, jnp.zeros((T, LANES), F32))
    inner[...] = jnp.broadcast_to(jnp.sum(jnp.transpose(acc), axis=0, keepdims=True), (8, LANES))


def signal_grad_body(
    grad_values, signal, hyena_q, s0, s1, s2, s3, i0, i1, i2, i3, grad_hyena_q, grad_signal
):
    inv_row = inv_rms_row((s0, s1, s2, s3))
    inner = i0[0:1, :] + i1[0:1, :] + i2[0:1, :] + i3[0:1, :]
    inv = column(inv_row)
    drop = column(inner * inv_row * inv_row / D)

    def step(tile, _):
        at = lanes_of(tile)
        sig = signal[:, at]
        hq = hyena_q[:, at].astype(F32)
        grad_mix = inv * (grad_values[:, at] - hq * sig * drop)
        grad_hyena_q[:, at] = (grad_mix * sig).astype(BF16)
        grad_signal[:, at] = (grad_mix * hq).astype(BF16)
        return 0

    lax.fori_loop(0, signal.shape[1] // LANES, step, 0)


def filter_body(info, flipped, grad_signal, out):
    mask = conv_mask(info, info[4] + T - 1, -1)
    lane_group = lax.broadcasted_iota(jnp.int32, (T, LANES), 1) // GROUP
    count = LANES // GROUP

    def step(tile, _):
        at = lanes_of(tile)
        gs = grad_signal[:, at].astype(F32)
        stacked = jnp.concatenate(
            [jnp.where(lane_group == g, gs, 0.0).astype(BF16) for g in range(count)], axis=0
        )
        full = lax.dot_general(
            stacked, flipped[:, at], (((1,), (1,)), ((), ())), preferred_element_type=F32
        )
        rows = []
        for g in range(count):
            corr = jnp.where(mask, full[g * T : (g + 1) * T], 0.0)
            aligned = pltpu.roll(corr, T + 1, 1, stride=1, stride_axis=0)
            rows.append(jnp.sum(aligned[:, :LANES], axis=0, keepdims=True))
        out[pl.ds(pl.multiple_of(tile * 8, 8), 8), :] = jnp.concatenate(rows, axis=0)
        return 0

    lax.fori_loop(0, grad_signal.shape[1] // LANES, step, 0)


def conv_back_body(info, grad_signal, right, hyena_k, hyena_v, table, grad_k, grad_v):
    mask = conv_mask(info, info[4])

    def step(tile, _):
        at = lanes_of(tile)
        window = jnp.concatenate([grad_signal[:, at], right[:, at]], axis=0)
        grad_kv = banded_matmul(table, mask, window, tile)
        grad_k[:, at] = (grad_kv * hyena_v[:, at].astype(F32)).astype(BF16)
        grad_v[:, at] = (grad_kv * hyena_k[:, at].astype(F32)).astype(BF16)
        return 0

    lax.fori_loop(0, hyena_k.shape[1] // LANES, step, 0)


def attend_body(
    prob, q, k0, k1, k2, v0, v1, v2, og, attn_out, grad_q, own, part1, part2
):
    scale = HEAD**-0.5
    over_keys = (((0,), (0,)), ((), ()))

    def step(h, _):
        at = lanes_of(h)
        keys = jnp.concatenate([k2[:, at], k1[:, at], k0[:, at]], axis=0)
        vals = jnp.concatenate([v2[:, at], v1[:, at], v0[:, at]], axis=0)
        p = prob[h]
        gp = lax.dot_general(vals, og[:, at], (((1,), (1,)), ((), ())), preferred_element_type=F32)
        delta = jnp.sum(p * gp, axis=0, keepdims=True)
        gs = (p * (gp - delta) * scale).astype(BF16)
        attn_out[:, at] = lax.dot_general(
            p.astype(BF16), vals, over_keys, preferred_element_type=F32
        ).astype(BF16)
        grad_q[:, at] = lax.dot_general(
            gs, keys, over_keys, preferred_element_type=F32
        ).astype(BF16)
        part = jnp.dot(gs, q[:, at], preferred_element_type=F32)
        part2[:, at] = part[:T].astype(BF16)
        part1[:, at] = part[T : 2 * T].astype(BF16)
        own[:, at] = part[2 * T :]
        return 0

    lax.fori_loop(0, q.shape[1] // HEAD, step, 0)


def over_sequence(x):
    def route(f):
        return [(i, f(i // 8, i % 8)) for i in range(32)]

    x = x + lax.ppermute(x, "mirror", [(0, 1), (1, 0)])
    x = x + sum(
        lax.ppermute(x, "context", route(lambda a, b, d=d: ((a + d) % 4) * 8 + b))
        for d in (1, 2, 3)
    )
    x = x + lax.ppermute(x, "context", route(lambda a, b: a * 8 + (b ^ 4)))
    return x + sum(
        lax.ppermute(x, "context", route(lambda a, b, d=d: a * 8 + (b ^ d))) for d in (1, 2, 3)
    )


def body(hyena_q, hyena_k, hyena_v, filters, norm_gain, attn_q, attn_k, out_grad, doc_lengths):
    rows, channels = hyena_q.shape
    heads = channels // HEAD
    big = (rows, channels)
    band_flops = 2 * (channels // GROUP) * T * 2 * T * LANES
    attn_flops = 2 * heads * 3 * T * T * HEAD
    offset = lax.axis_index(SEQ_AXES) * rows
    ends = [doc_lengths[0]]
    for i in range(1, 4):
        ends.append(ends[-1] + doc_lengths[i])
    info = jnp.stack(ends + [offset.astype(jnp.int32)])
    gain = norm_gain[None, :]

    kv = (hyena_k.astype(F32) * hyena_v.astype(F32)).astype(BF16)
    left = shifted(kv, 1)
    k1 = shifted(attn_k, 1)
    k2 = shifted(attn_k, 2)
    groups = filters.shape[0]
    wide = filters.astype(F32)
    back_table = jnp.concatenate([wide, jnp.zeros((groups, T), F32)], axis=1)
    fwd_table = jnp.concatenate(
        [jnp.zeros((groups, 1), F32), wide[:, ::-1], jnp.zeros((groups, T - 1), F32)], axis=1
    )
    signal, square, flipped = call(
        conv_body,
        (info, left, kv, hyena_q, fwd_table),
        (sds(*big), sds(8, LANES), sds(2 * rows, channels, dtype=BF16)),
        band_flops,
    )
    squares = [square] + [across(square, d) for d in (1, 2, 3)]
    (values,) = call(
        values_body,
        (signal, hyena_q, gain, *squares),
        (sds(*big, dtype=BF16),),
        4 * rows * channels,
    )
    prob, value_own, value1, value2 = call(
        scores_body,
        (info, attn_q, attn_k, k1, k2, out_grad),
        (sds(heads, 3 * T, T), sds(*big), sds(*big, dtype=BF16), sds(*big, dtype=BF16)),
        2 * attn_flops,
        exps=heads * 3 * T * T,
    )
    v1 = shifted(values, 1)
    v2 = shifted(values, 2)
    back1 = shifted(value1, -1)
    back2 = shifted(value2, -2)
    gain_grad, inner = call(
        inner_body,
        (value_own, back1, back2, signal, hyena_q, gain),
        (sds(*big), sds(8, LANES)),
        6 * rows * channels,
    )
    inners = [inner] + [across(inner, d) for d in (1, 2, 3)]
    grad_hyena_q, grad_signal = call(
        signal_grad_body,
        (gain_grad, signal, hyena_q, *squares, *inners),
        (sds(*big, dtype=BF16), sds(*big, dtype=BF16)),
        8 * rows * channels,
    )
    right = shifted(grad_signal, -1)
    (local,) = call(
        filter_body, (info, flipped, grad_signal), (sds(groups, LANES),), band_flops
    )
    grad_filters = over_sequence(local)
    attn_out, grad_attn_q, key_own, key1, key2 = call(
        attend_body,
        (prob, attn_q, attn_k, k1, k2, values, v1, v2, out_grad),
        (
            sds(*big, dtype=BF16),
            sds(*big, dtype=BF16),
            sds(*big),
            sds(*big, dtype=BF16),
            sds(*big, dtype=BF16),
        ),
        4 * attn_flops,
    )
    grad_attn_k = (
        key_own + shifted(key1, -1).astype(F32) + shifted(key2, -2).astype(F32)
    ).astype(BF16)
    grad_hyena_k, grad_hyena_v = call(
        conv_back_body,
        (info, grad_signal, right, hyena_k, hyena_v, back_table),
        (sds(*big, dtype=BF16), sds(*big, dtype=BF16)),
        band_flops,
    )
    return (
        attn_out,
        grad_attn_q,
        grad_attn_k,
        grad_hyena_q,
        grad_hyena_k,
        grad_hyena_v,
        grad_filters,
    )


def solution(mesh):
    tokens = P(SEQ_AXES, "tensor")
    return jax.shard_map(
        body,
        mesh=mesh,
        in_specs=(
            tokens,
            tokens,
            tokens,
            P("tensor", None),
            P("tensor"),
            tokens,
            tokens,
            tokens,
            P(),
        ),
        out_specs=(tokens, tokens, tokens, tokens, tokens, tokens, P("tensor", None)),
        check_vma=False,
    )
```

```python
import jax
import jax.numpy as jnp
from jax import lax
from jax.experimental import pallas as pl
from jax.experimental.pallas import tpu as pltpu
from jax.sharding import PartitionSpec as P


HEAD = 128
D = 8192
T = 128
LANES = 128
GROUP = 16
F32 = jnp.float32
BF16 = jnp.bfloat16
SEQ_AXES = ("context", "mirror")
UNROLL = 4

VMEM = pl.BlockSpec(memory_space=pltpu.VMEM)
SMEM = pl.BlockSpec(memory_space=pltpu.SMEM)


def shifted(block, distance):
    count = lax.axis_size(SEQ_AXES)
    route = [(i - distance, i) for i in range(count) if 0 <= i - distance < count]
    return lax.ppermute(block, SEQ_AXES, route)


def across(block):
    count = lax.axis_size("tensor")
    others = []
    for d in (2, 1, 3):
        route = [(i, (i + d) % count) for i in range(count)]
        others.append(lax.ppermute(block, "tensor", route))
    return [block] + others


def call(body, ins, outs, flops, room, exps=0):
    nbytes = sum(a.size * a.dtype.itemsize for a in ins)
    nbytes += sum(o.size * o.dtype.itemsize for o in outs)
    specs = [SMEM if a.dtype == jnp.int32 else VMEM for a in ins]
    return pl.pallas_call(
        body,
        out_shape=tuple(outs),
        in_specs=specs,
        out_specs=tuple(VMEM for _ in outs),
        compiler_params=pltpu.CompilerParams(vmem_limit_bytes=room << 20),
        cost_estimate=pl.CostEstimate(flops=flops, bytes_accessed=nbytes, transcendentals=exps),
    )(*ins)


def sds(*shape, dtype=F32):
    return jax.ShapeDtypeStruct(shape, dtype)


def doc_of(lengths, pos):
    end = lengths[0]
    doc = (pos >= end).astype(jnp.int32)
    for i in range(1, 4):
        end = end + lengths[i]
        doc = doc + (pos >= end).astype(jnp.int32)
    return doc


def conv_mask(lengths, own, first, sign=1):
    rows = own + lax.broadcasted_iota(jnp.int32, (T, 2 * T), 0)
    cols = first + sign * lax.broadcasted_iota(jnp.int32, (T, 2 * T), 1)
    return doc_of(lengths, rows) == doc_of(lengths, cols)


def column(row):
    return jnp.transpose(jnp.broadcast_to(row, (T, LANES)))


def banded_matmul(table_ref, mask, window, tile):
    bands = []
    for g in range(LANES // GROUP):
        row = table_ref[pl.ds(tile * 8 + g, 1), :]
        band = pltpu.roll(jnp.broadcast_to(row, (T, 2 * T)), 0, 1, stride=1, stride_axis=0)
        bands.append(jnp.where(mask, band, 0.0).astype(BF16))
    stacked = jnp.concatenate(bands, axis=0)
    full = jnp.dot(stacked, window, preferred_element_type=F32)
    lane_group = lax.broadcasted_iota(jnp.int32, (T, LANES), 1) // GROUP
    out = full[:T]
    for g in range(1, LANES // GROUP):
        out = jnp.where(lane_group == g, full[g * T : (g + 1) * T], out)
    return out


def lanes_of(tile):
    return pl.ds(pl.multiple_of(tile * LANES, LANES), LANES)


def conv_body(lengths, start, left, kv, hyena_q, table, signal, square, flipped):
    span = 2 * T
    turned = lax.broadcasted_iota(jnp.int32, (span, span), 0) + lax.broadcasted_iota(
        jnp.int32, (span, span), 1
    )
    turn = jnp.where(turned == span - 1, 1.0, 0.0).astype(BF16)
    mask = conv_mask(lengths, start[0], start[0] - T)
    tiles = kv.shape[1] // LANES

    def step(tile, acc):
        at = lanes_of(tile)
        window = jnp.concatenate([left[:, at], kv[:, at]], axis=0)
        out = banded_matmul(table, mask, window, tile)
        signal[:, at] = out
        flipped[:, at] = jnp.dot(turn, window, preferred_element_type=F32).astype(BF16)
        mix = hyena_q[:, at].astype(F32) * out
        return acc + mix * mix

    acc = lax.fori_loop(0, tiles, step, jnp.zeros((T, LANES), F32), unroll=UNROLL)
    square[...] = jnp.broadcast_to(jnp.sum(jnp.transpose(acc), axis=0, keepdims=True), (8, LANES))


def inv_rms_row(squares):
    total = squares[0][0:1, :]
    for s in squares[1:]:
        total = total + s[0:1, :]
    return lax.rsqrt(total / D + 1e-06)


def values_body(signal, hyena_q, gain, s0, s1, s2, s3, values):
    inv = column(inv_rms_row((s0, s1, s2, s3)))

    def step(tile, _):
        at = lanes_of(tile)
        mix = hyena_q[:, at].astype(F32) * signal[:, at]
        values[:, at] = (mix * inv * gain[:, at]).astype(BF16)
        return 0

    lax.fori_loop(0, signal.shape[1] // LANES, step, 0, unroll=UNROLL)


def scores_body(lengths, start, q, k0, k1, k2, og, prob, own, part1, part2):
    span = 3 * T
    query_pos = start[0] + lax.broadcasted_iota(jnp.int32, (span, T), 1)
    key_pos = start[0] - 2 * T + lax.broadcasted_iota(jnp.int32, (span, T), 0)
    allowed = (
        (key_pos >= 0)
        & (key_pos <= query_pos)
        & (query_pos - key_pos <= 2 * T)
        & (doc_of(lengths, key_pos) == doc_of(lengths, query_pos))
    )
    scale = HEAD**-0.5

    def step(h, _):
        at = lanes_of(h)
        keys = jnp.concatenate([k2[:, at], k1[:, at], k0[:, at]], axis=0)
        s = lax.dot_general(keys, q[:, at], (((1,), (1,)), ((), ())), preferred_element_type=F32)
        s = jnp.where(allowed, s * scale, -1e30)
        top = jnp.max(s, axis=0, keepdims=True)
        e = jnp.exp(s - top)
        p = e * (1.0 / jnp.sum(e, axis=0, keepdims=True))
        prob[h] = p
        part = jnp.dot(p.astype(BF16), og[:, at], preferred_element_type=F32)
        part2[:, at] = part[:T].astype(BF16)
        part1[:, at] = part[T : 2 * T].astype(BF16)
        own[:, at] = part[2 * T :]
        return 0

    lax.fori_loop(0, q.shape[1] // HEAD, step, 0, unroll=UNROLL)


def inner_body(own, part1, part2, signal, hyena_q, gain, grad_values, inner):
    def step(tile, acc):
        at = lanes_of(tile)
        gv = own[:, at] + part1[:, at].astype(F32) + part2[:, at].astype(F32)
        gv = gv * gain[:, at]
        grad_values[:, at] = gv
        return acc + gv * (hyena_q[:, at].astype(F32) * signal[:, at])

    acc = lax.fori_loop(0, own.shape[1] // LANES, step, jnp.zeros((T, LANES), F32), unroll=UNROLL)
    inner[...] = jnp.broadcast_to(jnp.sum(jnp.transpose(acc), axis=0, keepdims=True), (8, LANES))


def signal_grad_body(
    grad_values, signal, hyena_q, s0, s1, s2, s3, i0, i1, i2, i3, grad_hyena_q, grad_signal
):
    inv_row = inv_rms_row((s0, s1, s2, s3))
    inner = i0[0:1, :] + i1[0:1, :] + i2[0:1, :] + i3[0:1, :]
    inv = column(inv_row)
    drop = column(inner * inv_row * inv_row / D)

    def step(tile, _):
        at = lanes_of(tile)
        sig = signal[:, at]
        hq = hyena_q[:, at].astype(F32)
        grad_mix = inv * (grad_values[:, at] - hq * sig * drop)
        grad_hyena_q[:, at] = (grad_mix * sig).astype(BF16)
        grad_signal[:, at] = (grad_mix * hq).astype(BF16)
        return 0

    lax.fori_loop(0, signal.shape[1] // LANES, step, 0, unroll=UNROLL)


def filter_body(lengths, start, flipped, grad_signal, out):
    mask = conv_mask(lengths, start[0], start[0] + T - 1, -1)
    lane_group = lax.broadcasted_iota(jnp.int32, (T, LANES), 1) // GROUP
    count = LANES // GROUP

    def step(tile, _):
        at = lanes_of(tile)
        gs = grad_signal[:, at].astype(F32)
        stacked = jnp.concatenate(
            [jnp.where(lane_group == g, gs, 0.0).astype(BF16) for g in range(count)], axis=0
        )
        full = lax.dot_general(
            stacked, flipped[:, at], (((1,), (1,)), ((), ())), preferred_element_type=F32
        )
        rows = []
        for g in range(count):
            corr = jnp.where(mask, full[g * T : (g + 1) * T], 0.0)
            aligned = pltpu.roll(corr, T + 1, 1, stride=1, stride_axis=0)
            rows.append(jnp.sum(aligned[:, :LANES], axis=0, keepdims=True))
        out[pl.ds(pl.multiple_of(tile * 8, 8), 8), :] = jnp.concatenate(rows, axis=0)
        return 0

    lax.fori_loop(0, grad_signal.shape[1] // LANES, step, 0, unroll=UNROLL)


def conv_back_body(lengths, start, grad_signal, right, hyena_k, hyena_v, table, grad_k, grad_v):
    mask = conv_mask(lengths, start[0], start[0])

    def step(tile, _):
        at = lanes_of(tile)
        window = jnp.concatenate([grad_signal[:, at], right[:, at]], axis=0)
        grad_kv = banded_matmul(table, mask, window, tile)
        grad_k[:, at] = (grad_kv * hyena_v[:, at].astype(F32)).astype(BF16)
        grad_v[:, at] = (grad_kv * hyena_k[:, at].astype(F32)).astype(BF16)
        return 0

    lax.fori_loop(0, hyena_k.shape[1] // LANES, step, 0, unroll=UNROLL)


def attend_body(
    prob, q, k0, k1, k2, v0, v1, v2, og, attn_out, grad_q, own, part1, part2
):
    scale = HEAD**-0.5
    over_keys = (((0,), (0,)), ((), ()))

    def step(h, _):
        at = lanes_of(h)
        keys = jnp.concatenate([k2[:, at], k1[:, at], k0[:, at]], axis=0)
        vals = jnp.concatenate([v2[:, at], v1[:, at], v0[:, at]], axis=0)
        p = prob[h]
        gp = lax.dot_general(vals, og[:, at], (((1,), (1,)), ((), ())), preferred_element_type=F32)
        delta = jnp.sum(p * gp, axis=0, keepdims=True)
        gs = (p * (gp - delta) * scale).astype(BF16)
        attn_out[:, at] = lax.dot_general(
            p.astype(BF16), vals, over_keys, preferred_element_type=F32
        ).astype(BF16)
        grad_q[:, at] = lax.dot_general(
            gs, keys, over_keys, preferred_element_type=F32
        ).astype(BF16)
        part = jnp.dot(gs, q[:, at], preferred_element_type=F32)
        part2[:, at] = part[:T].astype(BF16)
        part1[:, at] = part[T : 2 * T].astype(BF16)
        own[:, at] = part[2 * T :]
        return 0

    lax.fori_loop(0, q.shape[1] // HEAD, step, 0, unroll=UNROLL)


def over_sequence(x):
    def send(x, f):
        return lax.ppermute(x, "context", [(i, f(i // 8, i % 8)) for i in range(32)])

    x = x + lax.ppermute(x, "mirror", [(0, 1), (1, 0)])
    parts = [send(x, lambda a, b, d=d: ((a + d) % 4) * 8 + b) for d in (2, 1, 3)]
    x = x + parts[0] + parts[1] + parts[2]
    x = x + send(x, lambda a, b: a * 8 + (b ^ 4))
    parts = [send(x, lambda a, b, d=d: a * 8 + (b ^ d)) for d in (3, 2, 1)]
    return x + parts[0] + parts[1] + parts[2]


def body(hyena_q, hyena_k, hyena_v, filters, norm_gain, attn_q, attn_k, out_grad, doc_lengths):
    rows, channels = hyena_q.shape
    heads = channels // HEAD
    big = (rows, channels)
    band_flops = 2 * (channels // GROUP) * T * 2 * T * LANES
    attn_flops = 2 * heads * 3 * T * T * HEAD
    start = (lax.axis_index(SEQ_AXES) * rows).astype(jnp.int32).reshape(1)
    at = (doc_lengths, start)
    gain = norm_gain[None, :]
    wide = sds(*big)
    half = sds(*big, dtype=BF16)
    small = sds(8, LANES)

    kv = (hyena_k.astype(F32) * hyena_v.astype(F32)).astype(BF16)
    left = shifted(kv, 1)
    k2 = shifted(attn_k, 2)
    k1 = shifted(attn_k, 1)
    groups = filters.shape[0]
    taps = filters.astype(F32)
    back_table = jnp.concatenate([taps, jnp.zeros((groups, T), F32)], axis=1)
    fwd_table = jnp.concatenate(
        [jnp.zeros((groups, 1), F32), taps[:, ::-1], jnp.zeros((groups, T - 1), F32)], axis=1
    )
    signal, square, flipped = call(
        conv_body,
        (*at, left, kv, hyena_q, fwd_table),
        (wide, small, sds(2 * rows, channels, dtype=BF16)),
        band_flops,
        8,
    )
    squares = across(square)
    prob, value_own, value1, value2 = call(
        scores_body,
        (*at, attn_q, attn_k, k1, k2, out_grad),
        (sds(heads, 3 * T, T), wide, half, half),
        2 * attn_flops,
        16,
        exps=heads * 3 * T * T,
    )
    back2 = shifted(value2, -2)
    back1 = shifted(value1, -1)
    (values,) = call(
        values_body, (signal, hyena_q, gain, *squares), (half,), 4 * rows * channels, 8
    )
    v2 = shifted(values, 2)
    v1 = shifted(values, 1)
    gain_grad, inner = call(
        inner_body,
        (value_own, back1, back2, signal, hyena_q, gain),
        (wide, small),
        6 * rows * channels,
        10,
    )
    inners = across(inner)
    attn_out, grad_attn_q, key_own, key1, key2 = call(
        attend_body,
        (prob, attn_q, attn_k, k1, k2, values, v1, v2, out_grad),
        (half, half, wide, half, half),
        4 * attn_flops,
        16,
    )
    from2 = shifted(key2, -2)
    from1 = shifted(key1, -1)
    grad_hyena_q, grad_signal = call(
        signal_grad_body,
        (gain_grad, signal, hyena_q, *squares, *inners),
        (half, half),
        8 * rows * channels,
        10,
    )
    right = shifted(grad_signal, -1)
    (local,) = call(filter_body, (*at, flipped, grad_signal), (sds(groups, LANES),), band_flops, 10)
    grad_filters = over_sequence(local)
    grad_attn_k = (key_own + from1.astype(F32) + from2.astype(F32)).astype(BF16)
    grad_hyena_k, grad_hyena_v = call(
        conv_back_body,
        (*at, grad_signal, right, hyena_k, hyena_v, back_table),
        (half, half),
        band_flops,
        10,
    )
    return (
        attn_out,
        grad_attn_q,
        grad_attn_k,
        grad_hyena_q,
        grad_hyena_k,
        grad_hyena_v,
        grad_filters,
    )


def solution(mesh):
    tokens = P(SEQ_AXES, "tensor")

    return jax.shard_map(
        body,
        mesh=mesh,
        in_specs=(
            tokens,
            tokens,
            tokens,
            P("tensor", None),
            P("tensor"),
            tokens,
            tokens,
            tokens,
            P(),
        ),
        out_specs=(tokens, tokens, tokens, tokens, tokens, tokens, P("tensor", None)),
        check_vma=False,
    )
```

```python
import jax
import jax.numpy as jnp
from jax import lax
from jax.experimental import pallas as pl
from jax.experimental.pallas import tpu as pltpu
from jax.sharding import PartitionSpec as P


HEAD = 128
D = 8192
T = 128
LANES = 128
GROUP = 16
F32 = jnp.float32
BF16 = jnp.bfloat16
SEQ_AXES = ("context", "mirror")
UNROLL = 4

VMEM = pl.BlockSpec(memory_space=pltpu.VMEM)
SMEM = pl.BlockSpec(memory_space=pltpu.SMEM)


def shifted(block, distance):
    count = lax.axis_size(SEQ_AXES)
    route = [(i, (i + distance) % count) for i in range(count)]
    return lax.ppermute(block, SEQ_AXES, route)


def across(block):
    count = lax.axis_size("tensor")
    others = []
    for d in (2, 1, 3):
        route = [(i, (i + d) % count) for i in range(count)]
        others.append(lax.ppermute(block, "tensor", route))
    return [block] + others


def call(body, ins, outs, flops, room, exps=0):
    nbytes = sum(a.size * a.dtype.itemsize for a in ins)
    nbytes += sum(o.size * o.dtype.itemsize for o in outs)
    specs = [SMEM if a.dtype == jnp.int32 else VMEM for a in ins]
    return pl.pallas_call(
        body,
        out_shape=tuple(outs),
        in_specs=specs,
        out_specs=tuple(VMEM for _ in outs),
        compiler_params=pltpu.CompilerParams(vmem_limit_bytes=room << 20),
        cost_estimate=pl.CostEstimate(flops=flops, bytes_accessed=nbytes, transcendentals=exps),
    )(*ins)


def sds(*shape, dtype=F32):
    return jax.ShapeDtypeStruct(shape, dtype)


def doc_of(lengths, pos):
    end = lengths[0]
    doc = (pos >= end).astype(jnp.int32)
    for i in range(1, 4):
        end = end + lengths[i]
        doc = doc + (pos >= end).astype(jnp.int32)
    return doc


def same_doc(lengths, own, cols):
    rows = own + lax.broadcasted_iota(jnp.int32, (T, T), 0)
    return (doc_of(lengths, rows) == doc_of(lengths, cols)) & (cols >= 0)


def half_masks(lengths, own, first):
    t = lax.broadcasted_iota(jnp.int32, (T, T), 0)
    l = lax.broadcasted_iota(jnp.int32, (T, T), 1)
    low, high = (l > t, l <= t) if first != 0 else (l >= t, l < t)
    masks = []
    for half, base in ((low, own + first), (high, own + first + T)):
        keep = half & same_doc(lengths, own, base + l)
        masks.append(jnp.where(keep, 1.0, 0.0).astype(BF16))
    return masks


def column(row):
    return jnp.transpose(jnp.broadcast_to(row, (T, LANES)))


def banded_matmul(table_ref, masks, window, tile):
    bands = []
    for g in range(LANES // GROUP):
        row = table_ref[pl.ds(tile * 8 + g, 1), :]
        turned = pltpu.roll(jnp.broadcast_to(row, (T, T)), 0, 1, stride=1, stride_axis=0)
        turned = turned.astype(BF16)
        bands.append(jnp.concatenate([turned * masks[0], turned * masks[1]], axis=1))
    stacked = jnp.concatenate(bands, axis=0)
    full = jnp.dot(stacked, window, preferred_element_type=F32)
    lane_group = lax.broadcasted_iota(jnp.int32, (T, LANES), 1) // GROUP
    out = full[:T]
    for g in range(1, LANES // GROUP):
        out = jnp.where(lane_group == g, full[g * T : (g + 1) * T], out)
    return out


def lanes_of(tile):
    return pl.ds(pl.multiple_of(tile * LANES, LANES), LANES)


def conv_body(lengths, start, left, kv, hyena_q, table, signal, square, flipped):
    span = 2 * T
    turned = lax.broadcasted_iota(jnp.int32, (span, span), 0) + lax.broadcasted_iota(
        jnp.int32, (span, span), 1
    )
    turn = jnp.where(turned == span - 1, 1.0, 0.0).astype(BF16)
    mask = half_masks(lengths, start[0], -T)
    tiles = kv.shape[1] // LANES

    def step(tile, acc):
        at = lanes_of(tile)
        window = jnp.concatenate([left[:, at], kv[:, at]], axis=0)
        out = banded_matmul(table, mask, window, tile)
        signal[:, at] = out
        flipped[:, at] = jnp.dot(turn, window, preferred_element_type=F32).astype(BF16)
        mix = hyena_q[:, at].astype(F32) * out
        return acc + mix * mix

    acc = lax.fori_loop(0, tiles, step, jnp.zeros((T, LANES), F32), unroll=UNROLL)
    square[...] = jnp.broadcast_to(jnp.sum(jnp.transpose(acc), axis=0, keepdims=True), (8, LANES))


def inv_rms_row(squares):
    total = squares[0][0:1, :]
    for s in squares[1:]:
        total = total + s[0:1, :]
    return lax.rsqrt(total / D + 1e-06)


def values_body(signal, hyena_q, gain, s0, s1, s2, s3, values):
    inv = column(inv_rms_row((s0, s1, s2, s3)))

    def step(tile, _):
        at = lanes_of(tile)
        mix = hyena_q[:, at].astype(F32) * signal[:, at]
        values[:, at] = (mix * inv * gain[:, at]).astype(BF16)
        return 0

    lax.fori_loop(0, signal.shape[1] // LANES, step, 0, unroll=UNROLL)


def scores_body(lengths, start, q, k0, k1, k2, og, prob, own, lse):
    span = 3 * T
    query_pos = start[0] + lax.broadcasted_iota(jnp.int32, (span, T), 1)
    key_pos = start[0] - 2 * T + lax.broadcasted_iota(jnp.int32, (span, T), 0)
    allowed = (
        (key_pos >= 0)
        & (key_pos <= query_pos)
        & (query_pos - key_pos <= 2 * T)
        & (doc_of(lengths, key_pos) == doc_of(lengths, query_pos))
    )
    scale = HEAD**-0.5

    def step(h, _):
        at = lanes_of(h)
        keys = jnp.concatenate([k2[:, at], k1[:, at], k0[:, at]], axis=0)
        s = lax.dot_general(keys, q[:, at], (((1,), (1,)), ((), ())), preferred_element_type=F32)
        s = jnp.where(allowed, s * scale, -1e30)
        top = jnp.max(s, axis=0, keepdims=True)
        e = jnp.exp(s - top)
        total = jnp.sum(e, axis=0, keepdims=True)
        p = e * (1.0 / total)
        prob[h] = p
        lse[pl.ds(h, 1), :] = top + jnp.log(total)
        own[:, at] = jnp.dot(p[2 * T :].astype(BF16), og[:, at], preferred_element_type=F32)
        return 0

    lax.fori_loop(0, q.shape[1] // HEAD, step, 0, unroll=UNROLL)


def later_body(
    lengths, start, k0, q1, q2, og1, og2, lse1, lse2, own, signal, hyena_q, gain, prob, grad_values, inner
):
    span = 2 * T
    query_pos = start[0] + T + lax.broadcasted_iota(jnp.int32, (T, span), 1)
    key_pos = start[0] + lax.broadcasted_iota(jnp.int32, (T, span), 0)
    allowed = (query_pos - key_pos <= 2 * T) & (
        doc_of(lengths, key_pos) == doc_of(lengths, query_pos)
    )
    scale = HEAD**-0.5

    def step(h, acc):
        at = lanes_of(h)
        queries = jnp.concatenate([q1[:, at], q2[:, at]], axis=0)
        grads = jnp.concatenate([og1[:, at], og2[:, at]], axis=0)
        row = jnp.concatenate([lse1[pl.ds(h, 1), :], lse2[pl.ds(h, 1), :]], axis=1)
        s = lax.dot_general(k0[:, at], queries, (((1,), (1,)), ((), ())), preferred_element_type=F32)
        p = jnp.exp(jnp.where(allowed, s * scale - row, -1e30))
        prob[h] = p
        gv = own[:, at] + jnp.dot(p.astype(BF16), grads, preferred_element_type=F32)
        gv = gv * gain[:, at]
        grad_values[:, at] = gv
        return acc + gv * (hyena_q[:, at].astype(F32) * signal[:, at])

    acc = lax.fori_loop(0, own.shape[1] // HEAD, step, jnp.zeros((T, LANES), F32), unroll=UNROLL)
    inner[...] = jnp.broadcast_to(jnp.sum(jnp.transpose(acc), axis=0, keepdims=True), (8, LANES))


def signal_grad_body(
    grad_values, signal, hyena_q, s0, s1, s2, s3, i0, i1, i2, i3, grad_hyena_q, grad_signal
):
    inv_row = inv_rms_row((s0, s1, s2, s3))
    inner = i0[0:1, :] + i1[0:1, :] + i2[0:1, :] + i3[0:1, :]
    inv = column(inv_row)
    drop = column(inner * inv_row * inv_row / D)

    def step(tile, _):
        at = lanes_of(tile)
        sig = signal[:, at]
        hq = hyena_q[:, at].astype(F32)
        grad_mix = inv * (grad_values[:, at] - hq * sig * drop)
        grad_hyena_q[:, at] = (grad_mix * sig).astype(BF16)
        grad_signal[:, at] = (grad_mix * hq).astype(BF16)
        return 0

    lax.fori_loop(0, signal.shape[1] // LANES, step, 0, unroll=UNROLL)


def filter_body(lengths, start, flipped, grad_signal, out):
    t = lax.broadcasted_iota(jnp.int32, (T, T), 0)
    l = lax.broadcasted_iota(jnp.int32, (T, T), 1)
    own = l >= T - 1 - t
    mask = same_doc(lengths, start[0], start[0] - 1 - l + jnp.where(own, T, 0))
    lane_group = lax.broadcasted_iota(jnp.int32, (T, LANES), 1) // GROUP
    count = LANES // GROUP

    def step(tile, _):
        at = lanes_of(tile)
        gs = grad_signal[:, at].astype(F32)
        stacked = jnp.concatenate(
            [jnp.where(lane_group == g, gs, 0.0).astype(BF16) for g in range(count)], axis=0
        )
        full = lax.dot_general(
            stacked, flipped[:, at], (((1,), (1,)), ((), ())), preferred_element_type=F32
        )
        rows = []
        for g in range(count):
            corr = full[g * T : (g + 1) * T]
            corr = jnp.where(mask, jnp.where(own, corr[:, :T], corr[:, T:]), 0.0)
            aligned = pltpu.roll(corr, 1, 1, stride=1, stride_axis=0)
            rows.append(jnp.sum(aligned, axis=0, keepdims=True))
        out[pl.ds(pl.multiple_of(tile * 8, 8), 8), :] = jnp.concatenate(rows, axis=0)
        return 0

    lax.fori_loop(0, grad_signal.shape[1] // LANES, step, 0, unroll=UNROLL)


def conv_back_body(lengths, start, grad_signal, right, hyena_k, hyena_v, table, grad_k, grad_v):
    mask = half_masks(lengths, start[0], 0)

    def step(tile, _):
        at = lanes_of(tile)
        window = jnp.concatenate([grad_signal[:, at], right[:, at]], axis=0)
        grad_kv = banded_matmul(table, mask, window, tile)
        grad_k[:, at] = (grad_kv * hyena_v[:, at].astype(F32)).astype(BF16)
        grad_v[:, at] = (grad_kv * hyena_k[:, at].astype(F32)).astype(BF16)
        return 0

    lax.fori_loop(0, hyena_k.shape[1] // LANES, step, 0, unroll=UNROLL)


def attend_body(
    prob, q, k0, k1, k2, v0, v1, v2, og, attn_out, grad_q, own, delta_rows
):
    scale = HEAD**-0.5
    over_keys = (((0,), (0,)), ((), ()))

    def step(h, _):
        at = lanes_of(h)
        keys = jnp.concatenate([k2[:, at], k1[:, at], k0[:, at]], axis=0)
        vals = jnp.concatenate([v2[:, at], v1[:, at], v0[:, at]], axis=0)
        p = prob[h]
        gp = lax.dot_general(vals, og[:, at], (((1,), (1,)), ((), ())), preferred_element_type=F32)
        delta = jnp.sum(p * gp, axis=0, keepdims=True)
        delta_rows[pl.ds(h, 1), :] = delta
        gs = (p * (gp - delta) * scale).astype(BF16)
        attn_out[:, at] = lax.dot_general(
            p.astype(BF16), vals, over_keys, preferred_element_type=F32
        ).astype(BF16)
        grad_q[:, at] = lax.dot_general(
            gs, keys, over_keys, preferred_element_type=F32
        ).astype(BF16)
        own[:, at] = jnp.dot(gs[2 * T :], q[:, at], preferred_element_type=F32)
        return 0

    lax.fori_loop(0, q.shape[1] // HEAD, step, 0, unroll=UNROLL)


def keys_body(prob, v0, q1, q2, og1, og2, delta1, delta2, own, grad_k):
    scale = HEAD**-0.5

    def step(h, _):
        at = lanes_of(h)
        queries = jnp.concatenate([q1[:, at], q2[:, at]], axis=0)
        grads = jnp.concatenate([og1[:, at], og2[:, at]], axis=0)
        delta = jnp.concatenate([delta1[pl.ds(h, 1), :], delta2[pl.ds(h, 1), :]], axis=1)
        gp = lax.dot_general(v0[:, at], grads, (((1,), (1,)), ((), ())), preferred_element_type=F32)
        gs = (prob[h] * (gp - delta) * scale).astype(BF16)
        part = jnp.dot(gs, queries, preferred_element_type=F32)
        grad_k[:, at] = (own[:, at] + part).astype(BF16)
        return 0

    lax.fori_loop(0, v0.shape[1] // HEAD, step, 0, unroll=UNROLL)


def over_sequence(x):
    def send(x, f):
        return lax.ppermute(x, "context", [(i, f(i // 8, i % 8)) for i in range(32)])

    x = x + lax.ppermute(x, "mirror", [(0, 1), (1, 0)])
    parts = [send(x, lambda a, b, d=d: ((a + d) % 4) * 8 + b) for d in (2, 1, 3)]
    x = x + parts[0] + parts[1] + parts[2]
    x = x + send(x, lambda a, b: a * 8 + (b ^ 4))
    parts = [send(x, lambda a, b, d=d: a * 8 + (b ^ d)) for d in (3, 2, 1)]
    return x + parts[0] + parts[1] + parts[2]


def body(hyena_q, hyena_k, hyena_v, filters, norm_gain, attn_q, attn_k, out_grad, doc_lengths):
    rows, channels = hyena_q.shape
    heads = channels // HEAD
    big = (rows, channels)
    band_flops = 2 * (channels // GROUP) * T * 2 * T * LANES
    attn_flops = 2 * heads * 3 * T * T * HEAD
    start = (lax.axis_index(SEQ_AXES) * rows).astype(jnp.int32).reshape(1)
    at = (doc_lengths, start)
    gain = norm_gain[None, :]
    wide = sds(*big)
    half = sds(*big, dtype=BF16)
    small = sds(8, LANES)

    kv = (hyena_k.astype(F32) * hyena_v.astype(F32)).astype(BF16)
    left = shifted(kv, 1)
    og2 = shifted(out_grad, -2)
    q2 = shifted(attn_q, -2)
    og1 = shifted(out_grad, -1)
    q1 = shifted(attn_q, -1)
    k2 = shifted(attn_k, 2)
    k1 = shifted(attn_k, 1)
    groups = filters.shape[0]
    taps = filters.astype(F32)
    fwd_taps = jnp.concatenate([taps[:, :1], taps[:, :0:-1]], axis=1)
    signal, square, flipped = call(
        conv_body,
        (*at, left, kv, hyena_q, fwd_taps),
        (wide, small, sds(2 * rows, channels, dtype=BF16)),
        band_flops,
        8,
    )
    squares = across(square)
    stat = sds(heads, T)
    prob, value_own, lse = call(
        scores_body,
        (*at, attn_q, attn_k, k1, k2, out_grad),
        (sds(heads, 3 * T, T), wide, stat),
        4 * attn_flops // 3,
        16,
        exps=heads * 3 * T * T,
    )
    lse2 = shifted(lse, -2)
    lse1 = shifted(lse, -1)
    (values,) = call(
        values_body, (signal, hyena_q, gain, *squares), (half,), 4 * rows * channels, 8
    )
    v2 = shifted(values, 2)
    v1 = shifted(values, 1)
    prob_later, gain_grad, inner = call(
        later_body,
        (*at, attn_k, q1, q2, og1, og2, lse1, lse2, value_own, signal, hyena_q, gain),
        (sds(heads, T, 2 * T), wide, small),
        4 * attn_flops // 3,
        14,
        exps=heads * 2 * T * T,
    )
    inners = across(inner)
    attn_out, grad_attn_q, key_own, delta = call(
        attend_body,
        (prob, attn_q, attn_k, k1, k2, values, v1, v2, out_grad),
        (half, half, wide, stat),
        10 * attn_flops // 3,
        16,
    )
    delta2 = shifted(delta, -2)
    delta1 = shifted(delta, -1)
    grad_hyena_q, grad_signal = call(
        signal_grad_body,
        (gain_grad, signal, hyena_q, *squares, *inners),
        (half, half),
        8 * rows * channels,
        10,
    )
    right = shifted(grad_signal, -1)
    (local,) = call(filter_body, (*at, flipped, grad_signal), (sds(groups, LANES),), band_flops, 10)
    grad_filters = over_sequence(local)
    (grad_attn_k,) = call(
        keys_body,
        (prob_later, values, q1, q2, og1, og2, delta1, delta2, key_own),
        (half,),
        4 * attn_flops // 3,
        12,
    )
    grad_hyena_k, grad_hyena_v = call(
        conv_back_body,
        (*at, grad_signal, right, hyena_k, hyena_v, taps),
        (half, half),
        band_flops,
        10,
    )
    return (
        attn_out,
        grad_attn_q,
        grad_attn_k,
        grad_hyena_q,
        grad_hyena_k,
        grad_hyena_v,
        grad_filters,
    )


def solution(mesh):
    tokens = P(SEQ_AXES, "tensor")

    return jax.shard_map(
        body,
        mesh=mesh,
        in_specs=(
            tokens,
            tokens,
            tokens,
            P("tensor", None),
            P("tensor"),
            tokens,
            tokens,
            tokens,
            P(),
        ),
        out_specs=(tokens, tokens, tokens, tokens, tokens, tokens, P("tensor", None)),
        check_vma=False,
    )
```

```python
import jax
import jax.numpy as jnp
from jax import lax
from jax.experimental import pallas as pl
from jax.experimental.pallas import tpu as pltpu
from jax.sharding import PartitionSpec as P


HEAD = 128
D = 8192
T = 128
LANES = 128
GROUP = 16
F32 = jnp.float32
BF16 = jnp.bfloat16
SEQ_AXES = ("context", "mirror")
UNROLL = 4

VMEM = pl.BlockSpec(memory_space=pltpu.VMEM)
SMEM = pl.BlockSpec(memory_space=pltpu.SMEM)


def shifted(block, distance):
    count = lax.axis_size(SEQ_AXES)
    route = [(i, (i + distance) % count) for i in range(count)]
    return lax.ppermute(block, SEQ_AXES, route)


def across(block):
    count = lax.axis_size("tensor")
    others = []
    for d in (2, 1, 3):
        route = [(i, (i + d) % count) for i in range(count)]
        others.append(lax.ppermute(block, "tensor", route))
    return [block] + others


def call(body, ins, outs, flops, room, exps=0):
    nbytes = sum(a.size * a.dtype.itemsize for a in ins)
    nbytes += sum(o.size * o.dtype.itemsize for o in outs)
    specs = [SMEM if a.dtype == jnp.int32 else VMEM for a in ins]
    return pl.pallas_call(
        body,
        out_shape=tuple(outs),
        in_specs=specs,
        out_specs=tuple(VMEM for _ in outs),
        compiler_params=pltpu.CompilerParams(vmem_limit_bytes=room << 20),
        cost_estimate=pl.CostEstimate(flops=flops, bytes_accessed=nbytes, transcendentals=exps),
    )(*ins)


def sds(*shape, dtype=F32):
    return jax.ShapeDtypeStruct(shape, dtype)


def doc_of(lengths, pos):
    end = lengths[0]
    doc = (pos >= end).astype(jnp.int32)
    for i in range(1, 4):
        end = end + lengths[i]
        doc = doc + (pos >= end).astype(jnp.int32)
    return doc


def same_doc(lengths, own, cols):
    rows = own + lax.broadcasted_iota(jnp.int32, (T, T), 0)
    return (doc_of(lengths, rows) == doc_of(lengths, cols)) & (cols >= 0)


def half_masks(lengths, own, first):
    t = lax.broadcasted_iota(jnp.int32, (T, T), 0)
    l = lax.broadcasted_iota(jnp.int32, (T, T), 1)
    low, high = (l > t, l <= t) if first != 0 else (l >= t, l < t)
    masks = []
    for half, base in ((low, own + first), (high, own + first + T)):
        keep = half & same_doc(lengths, own, base + l)
        masks.append(jnp.where(keep, 1.0, 0.0).astype(BF16))
    return masks


def column(row):
    return jnp.transpose(jnp.broadcast_to(row, (T, LANES)))


def banded_matmul(table_ref, masks, window, tile):
    bands = []
    for g in range(LANES // GROUP):
        row = table_ref[pl.ds(tile * 8 + g, 1), :]
        turned = pltpu.roll(jnp.broadcast_to(row, (T, T)), 0, 1, stride=1, stride_axis=0)
        turned = turned.astype(BF16)
        bands.append(jnp.concatenate([turned * masks[0], turned * masks[1]], axis=1))
    stacked = jnp.concatenate(bands, axis=0)
    full = jnp.dot(stacked, window, preferred_element_type=F32)
    lane_group = lax.broadcasted_iota(jnp.int32, (T, LANES), 1) // GROUP
    out = full[:T]
    for g in range(1, LANES // GROUP):
        out = jnp.where(lane_group == g, full[g * T : (g + 1) * T], out)
    return out


def lanes_of(tile):
    return pl.ds(pl.multiple_of(tile * LANES, LANES), LANES)


def conv_body(lengths, start, left, kv, hyena_q, table, signal, square, flipped):
    span = 2 * T
    turned = lax.broadcasted_iota(jnp.int32, (span, span), 0) + lax.broadcasted_iota(
        jnp.int32, (span, span), 1
    )
    turn = jnp.where(turned == span - 1, 1.0, 0.0).astype(BF16)
    mask = half_masks(lengths, start[0], -T)
    tiles = kv.shape[1] // LANES

    def step(tile, acc):
        at = lanes_of(tile)
        window = jnp.concatenate([left[:, at], kv[:, at]], axis=0)
        out = banded_matmul(table, mask, window, tile)
        signal[:, at] = out
        flipped[:, at] = jnp.dot(turn, window, preferred_element_type=F32).astype(BF16)
        mix = hyena_q[:, at].astype(F32) * out
        return acc + mix * mix

    acc = lax.fori_loop(0, tiles, step, jnp.zeros((T, LANES), F32), unroll=UNROLL)
    square[...] = jnp.broadcast_to(jnp.sum(jnp.transpose(acc), axis=0, keepdims=True), (8, LANES))


def inv_rms_row(squares):
    total = squares[0][0:1, :]
    for s in squares[1:]:
        total = total + s[0:1, :]
    return lax.rsqrt(total / D + 1e-06)


def values_body(signal, hyena_q, gain, s0, s1, s2, s3, values):
    inv = column(inv_rms_row((s0, s1, s2, s3)))

    def step(tile, _):
        at = lanes_of(tile)
        mix = hyena_q[:, at].astype(F32) * signal[:, at]
        values[:, at] = (mix * inv * gain[:, at]).astype(BF16)
        return 0

    lax.fori_loop(0, signal.shape[1] // LANES, step, 0, unroll=UNROLL)


def scores_body(lengths, start, q, k0, k1, k2, og, prob, own, lse):
    span = 3 * T
    query_pos = start[0] + lax.broadcasted_iota(jnp.int32, (span, T), 1)
    key_pos = start[0] - 2 * T + lax.broadcasted_iota(jnp.int32, (span, T), 0)
    allowed = (
        (key_pos >= 0)
        & (key_pos <= query_pos)
        & (query_pos - key_pos <= 2 * T)
        & (doc_of(lengths, key_pos) == doc_of(lengths, query_pos))
    )
    scale = HEAD**-0.5

    def step(h, _):
        at = lanes_of(h)
        keys = jnp.concatenate([k2[:, at], k1[:, at], k0[:, at]], axis=0)
        s = lax.dot_general(keys, q[:, at], (((1,), (1,)), ((), ())), preferred_element_type=F32)
        s = jnp.where(allowed, s * scale, -1e30)
        top = jnp.max(s, axis=0, keepdims=True)
        e = jnp.exp(s - top)
        total = jnp.sum(e, axis=0, keepdims=True)
        p = e * (1.0 / total)
        prob[h] = p
        lse[pl.ds(h, 1), :] = top + jnp.log(total)
        own[:, at] = jnp.dot(p[2 * T :].astype(BF16), og[:, at], preferred_element_type=F32)
        return 0

    lax.fori_loop(0, q.shape[1] // HEAD, step, 0, unroll=UNROLL)


def later_body(
    lengths, start, k0, q1, q2, og1, og2, lse1, lse2, own, signal, hyena_q, gain, prob, grad_values, inner
):
    span = 2 * T
    query_pos = start[0] + T + lax.broadcasted_iota(jnp.int32, (T, span), 1)
    key_pos = start[0] + lax.broadcasted_iota(jnp.int32, (T, span), 0)
    allowed = (query_pos - key_pos <= 2 * T) & (
        doc_of(lengths, key_pos) == doc_of(lengths, query_pos)
    )
    scale = HEAD**-0.5

    def step(h, acc):
        at = lanes_of(h)
        queries = jnp.concatenate([q1[:, at], q2[:, at]], axis=0)
        grads = jnp.concatenate([og1[:, at], og2[:, at]], axis=0)
        row = jnp.concatenate([lse1[pl.ds(h, 1), :], lse2[pl.ds(h, 1), :]], axis=1)
        s = lax.dot_general(k0[:, at], queries, (((1,), (1,)), ((), ())), preferred_element_type=F32)
        p = jnp.exp(jnp.where(allowed, s * scale - row, -1e30))
        prob[h] = p
        gv = own[:, at] + jnp.dot(p.astype(BF16), grads, preferred_element_type=F32)
        gv = gv * gain[:, at]
        grad_values[:, at] = gv
        return acc + gv * (hyena_q[:, at].astype(F32) * signal[:, at])

    acc = lax.fori_loop(0, own.shape[1] // HEAD, step, jnp.zeros((T, LANES), F32), unroll=UNROLL)
    inner[...] = jnp.broadcast_to(jnp.sum(jnp.transpose(acc), axis=0, keepdims=True), (8, LANES))


def signal_grad_body(
    grad_values, signal, hyena_q, s0, s1, s2, s3, i0, i1, i2, i3, grad_hyena_q, grad_signal
):
    inv_row = inv_rms_row((s0, s1, s2, s3))
    inner = i0[0:1, :] + i1[0:1, :] + i2[0:1, :] + i3[0:1, :]
    inv = column(inv_row)
    drop = column(inner * inv_row * inv_row / D)

    def step(tile, _):
        at = lanes_of(tile)
        sig = signal[:, at]
        hq = hyena_q[:, at].astype(F32)
        grad_mix = inv * (grad_values[:, at] - hq * sig * drop)
        grad_hyena_q[:, at] = (grad_mix * sig).astype(BF16)
        grad_signal[:, at] = (grad_mix * hq).astype(BF16)
        return 0

    lax.fori_loop(0, signal.shape[1] // LANES, step, 0, unroll=UNROLL)


def filter_body(lengths, start, flipped, grad_signal, out):
    t = lax.broadcasted_iota(jnp.int32, (T, T), 0)
    l = lax.broadcasted_iota(jnp.int32, (T, T), 1)
    own = l >= T - 1 - t
    mask = same_doc(lengths, start[0], start[0] - 1 - l + jnp.where(own, T, 0))
    lane_group = lax.broadcasted_iota(jnp.int32, (T, LANES), 1) // GROUP
    count = LANES // GROUP

    def step(tile, _):
        at = lanes_of(tile)
        gs = grad_signal[:, at].astype(F32)
        stacked = jnp.concatenate(
            [jnp.where(lane_group == g, gs, 0.0).astype(BF16) for g in range(count)], axis=0
        )
        full = lax.dot_general(
            stacked, flipped[:, at], (((1,), (1,)), ((), ())), preferred_element_type=F32
        )
        rows = []
        for g in range(count):
            corr = full[g * T : (g + 1) * T]
            corr = jnp.where(mask, jnp.where(own, corr[:, :T], corr[:, T:]), 0.0)
            aligned = pltpu.roll(corr, 1, 1, stride=1, stride_axis=0)
            rows.append(jnp.sum(aligned, axis=0, keepdims=True))
        out[pl.ds(pl.multiple_of(tile * 8, 8), 8), :] = jnp.concatenate(rows, axis=0)
        return 0

    lax.fori_loop(0, grad_signal.shape[1] // LANES, step, 0, unroll=2 * UNROLL)


def conv_back_body(lengths, start, grad_signal, right, hyena_k, hyena_v, table, grad_k, grad_v):
    mask = half_masks(lengths, start[0], 0)

    def step(tile, _):
        at = lanes_of(tile)
        window = jnp.concatenate([grad_signal[:, at], right[:, at]], axis=0)
        grad_kv = banded_matmul(table, mask, window, tile)
        grad_k[:, at] = (grad_kv * hyena_v[:, at].astype(F32)).astype(BF16)
        grad_v[:, at] = (grad_kv * hyena_k[:, at].astype(F32)).astype(BF16)
        return 0

    lax.fori_loop(0, hyena_k.shape[1] // LANES, step, 0, unroll=UNROLL)


def delta_body(prob, q, v0, v1, v2, og, own, delta_rows):
    scale = HEAD**-0.5

    def step(h, _):
        at = lanes_of(h)
        vals = jnp.concatenate([v2[:, at], v1[:, at], v0[:, at]], axis=0)
        p = prob[h]
        gp = lax.dot_general(vals, og[:, at], (((1,), (1,)), ((), ())), preferred_element_type=F32)
        delta = jnp.sum(p * gp, axis=0, keepdims=True)
        delta_rows[pl.ds(h, 1), :] = delta
        gs = (p[2 * T :] * (gp[2 * T :] - delta) * scale).astype(BF16)
        own[:, at] = jnp.dot(gs, q[:, at], preferred_element_type=F32)
        return 0

    lax.fori_loop(0, q.shape[1] // HEAD, step, 0, unroll=UNROLL)


def out_body(prob, k0, k1, k2, v0, v1, v2, og, delta_rows, attn_out, grad_q):
    scale = HEAD**-0.5
    over_keys = (((0,), (0,)), ((), ()))

    def step(h, _):
        at = lanes_of(h)
        keys = jnp.concatenate([k2[:, at], k1[:, at], k0[:, at]], axis=0)
        vals = jnp.concatenate([v2[:, at], v1[:, at], v0[:, at]], axis=0)
        p = prob[h]
        gp = lax.dot_general(vals, og[:, at], (((1,), (1,)), ((), ())), preferred_element_type=F32)
        gs = (p * (gp - delta_rows[pl.ds(h, 1), :]) * scale).astype(BF16)
        attn_out[:, at] = lax.dot_general(
            p.astype(BF16), vals, over_keys, preferred_element_type=F32
        ).astype(BF16)
        grad_q[:, at] = lax.dot_general(
            gs, keys, over_keys, preferred_element_type=F32
        ).astype(BF16)
        return 0

    lax.fori_loop(0, k0.shape[1] // HEAD, step, 0, unroll=2 * UNROLL)


def keys_body(prob, v0, q1, q2, og1, og2, delta1, delta2, own, grad_k):
    scale = HEAD**-0.5

    def step(h, _):
        at = lanes_of(h)
        queries = jnp.concatenate([q1[:, at], q2[:, at]], axis=0)
        grads = jnp.concatenate([og1[:, at], og2[:, at]], axis=0)
        delta = jnp.concatenate([delta1[pl.ds(h, 1), :], delta2[pl.ds(h, 1), :]], axis=1)
        gp = lax.dot_general(v0[:, at], grads, (((1,), (1,)), ((), ())), preferred_element_type=F32)
        gs = (prob[h] * (gp - delta) * scale).astype(BF16)
        part = jnp.dot(gs, queries, preferred_element_type=F32)
        grad_k[:, at] = (own[:, at] + part).astype(BF16)
        return 0

    lax.fori_loop(0, v0.shape[1] // HEAD, step, 0, unroll=UNROLL)


def over_sequence(x):
    def send(x, f):
        return lax.ppermute(x, "context", [(i, f(i // 8, i % 8)) for i in range(32)])

    x = x + lax.ppermute(x, "mirror", [(0, 1), (1, 0)])
    parts = [send(x, lambda a, b, d=d: ((a + d) % 4) * 8 + b) for d in (2, 1, 3)]
    x = x + parts[0] + parts[1] + parts[2]
    x = x + send(x, lambda a, b: a * 8 + (b ^ 4))
    parts = [send(x, lambda a, b, d=d: a * 8 + (b ^ d)) for d in (3, 2, 1)]
    return x + parts[0] + parts[1] + parts[2]


def body(hyena_q, hyena_k, hyena_v, filters, norm_gain, attn_q, attn_k, out_grad, doc_lengths):
    rows, channels = hyena_q.shape
    heads = channels // HEAD
    big = (rows, channels)
    band_flops = 2 * (channels // GROUP) * T * 2 * T * LANES
    attn_flops = 2 * heads * 3 * T * T * HEAD
    start = (lax.axis_index(SEQ_AXES) * rows).astype(jnp.int32).reshape(1)
    at = (doc_lengths, start)
    gain = norm_gain[None, :]
    wide = sds(*big)
    half = sds(*big, dtype=BF16)
    small = sds(8, LANES)

    kv = (hyena_k.astype(F32) * hyena_v.astype(F32)).astype(BF16)
    left = shifted(kv, 1)
    og2 = shifted(out_grad, -2)
    q2 = shifted(attn_q, -2)
    og1 = shifted(out_grad, -1)
    q1 = shifted(attn_q, -1)
    k2 = shifted(attn_k, 2)
    k1 = shifted(attn_k, 1)
    groups = filters.shape[0]
    taps = filters.astype(F32)
    fwd_taps = jnp.concatenate([taps[:, :1], taps[:, :0:-1]], axis=1)
    signal, square, flipped = call(
        conv_body,
        (*at, left, kv, hyena_q, fwd_taps),
        (wide, small, sds(2 * rows, channels, dtype=BF16)),
        band_flops,
        8,
    )
    squares = across(square)
    stat = sds(heads, T)
    prob, value_own, lse = call(
        scores_body,
        (*at, attn_q, attn_k, k1, k2, out_grad),
        (sds(heads, 3 * T, T), wide, stat),
        4 * attn_flops // 3,
        16,
        exps=heads * 3 * T * T,
    )
    lse2 = shifted(lse, -2)
    lse1 = shifted(lse, -1)
    (values,) = call(
        values_body, (signal, hyena_q, gain, *squares), (half,), 4 * rows * channels, 8
    )
    v2 = shifted(values, 2)
    v1 = shifted(values, 1)
    prob_later, gain_grad, inner = call(
        later_body,
        (*at, attn_k, q1, q2, og1, og2, lse1, lse2, value_own, signal, hyena_q, gain),
        (sds(heads, T, 2 * T), wide, small),
        4 * attn_flops // 3,
        14,
        exps=heads * 2 * T * T,
    )
    inners = across(inner)
    key_own, delta = call(
        delta_body, (prob, attn_q, values, v1, v2, out_grad), (wide, stat), 4 * attn_flops // 3, 12
    )
    delta2 = shifted(delta, -2)
    delta1 = shifted(delta, -1)
    grad_hyena_q, grad_signal = call(
        signal_grad_body,
        (gain_grad, signal, hyena_q, *squares, *inners),
        (half, half),
        8 * rows * channels,
        10,
    )
    right = shifted(grad_signal, -1)
    (local,) = call(filter_body, (*at, flipped, grad_signal), (sds(groups, LANES),), band_flops, 10)
    grad_filters = over_sequence(local)
    (grad_attn_k,) = call(
        keys_body,
        (prob_later, values, q1, q2, og1, og2, delta1, delta2, key_own),
        (half,),
        4 * attn_flops // 3,
        12,
    )
    grad_hyena_k, grad_hyena_v = call(
        conv_back_body,
        (*at, grad_signal, right, hyena_k, hyena_v, taps),
        (half, half),
        band_flops,
        10,
    )
    attn_out, grad_attn_q = call(
        out_body,
        (prob, attn_k, k1, k2, values, v1, v2, out_grad, delta),
        (half, half),
        3 * attn_flops,
        14,
    )
    return (
        attn_out,
        grad_attn_q,
        grad_attn_k,
        grad_hyena_q,
        grad_hyena_k,
        grad_hyena_v,
        grad_filters,
    )


def solution(mesh):
    tokens = P(SEQ_AXES, "tensor")

    return jax.shard_map(
        body,
        mesh=mesh,
        in_specs=(
            tokens,
            tokens,
            tokens,
            P("tensor", None),
            P("tensor"),
            tokens,
            tokens,
            tokens,
            P(),
        ),
        out_specs=(tokens, tokens, tokens, tokens, tokens, tokens, P("tensor", None)),
        check_vma=False,
    )
```

```python
import jax
import jax.numpy as jnp
from jax import lax
from jax.experimental import pallas as pl
from jax.experimental.pallas import tpu as pltpu
from jax.sharding import PartitionSpec as P


HEAD = 128
D = 8192
T = 128
LANES = 128
GROUP = 16
F32 = jnp.float32
BF16 = jnp.bfloat16
SEQ_AXES = ("context", "mirror")
UNROLL = 4

VMEM = pl.BlockSpec(memory_space=pltpu.VMEM)
SMEM = pl.BlockSpec(memory_space=pltpu.SMEM)


def shifted(block, distance):
    count = lax.axis_size(SEQ_AXES)
    route = [(i, (i + distance) % count) for i in range(count)]
    return lax.ppermute(block, SEQ_AXES, route)


def across(block):
    count = lax.axis_size("tensor")
    others = []
    for d in (2, 1, 3):
        route = [(i, (i + d) % count) for i in range(count)]
        others.append(lax.ppermute(block, "tensor", route))
    return [block] + others


def call(body, ins, outs, flops, room, exps=0):
    nbytes = sum(a.size * a.dtype.itemsize for a in ins)
    nbytes += sum(o.size * o.dtype.itemsize for o in outs)
    specs = [SMEM if a.dtype == jnp.int32 else VMEM for a in ins]
    return pl.pallas_call(
        body,
        out_shape=tuple(outs),
        in_specs=specs,
        out_specs=tuple(VMEM for _ in outs),
        compiler_params=pltpu.CompilerParams(vmem_limit_bytes=room << 20),
        cost_estimate=pl.CostEstimate(flops=flops, bytes_accessed=nbytes, transcendentals=exps),
    )(*ins)


def sds(*shape, dtype=F32):
    return jax.ShapeDtypeStruct(shape, dtype)


def doc_of(lengths, pos):
    end = lengths[0]
    doc = (pos >= end).astype(jnp.int32)
    for i in range(1, 4):
        end = end + lengths[i]
        doc = doc + (pos >= end).astype(jnp.int32)
    return doc


def same_doc(lengths, own, cols):
    rows = own + lax.broadcasted_iota(jnp.int32, (T, T), 0)
    return (doc_of(lengths, rows) == doc_of(lengths, cols)) & (cols >= 0)


def half_masks(lengths, own, first):
    t = lax.broadcasted_iota(jnp.int32, (T, T), 0)
    l = lax.broadcasted_iota(jnp.int32, (T, T), 1)
    low, high = (l > t, l <= t) if first != 0 else (l >= t, l < t)
    masks = []
    for half, base in ((low, own + first), (high, own + first + T)):
        keep = half & same_doc(lengths, own, base + l)
        masks.append(jnp.where(keep, 1.0, 0.0).astype(BF16))
    return masks


def column(row):
    return jnp.transpose(jnp.broadcast_to(row, (T, LANES)))


def banded_matmul(table_ref, masks, window, tile):
    bands = []
    for g in range(LANES // GROUP):
        row = table_ref[pl.ds(tile * 8 + g, 1), :]
        turned = pltpu.roll(jnp.broadcast_to(row, (T, T)), 0, 1, stride=1, stride_axis=0)
        turned = turned.astype(BF16)
        bands.append(jnp.concatenate([turned * masks[0], turned * masks[1]], axis=1))
    stacked = jnp.concatenate(bands, axis=0)
    full = jnp.dot(stacked, window, preferred_element_type=F32)
    lane_group = lax.broadcasted_iota(jnp.int32, (T, LANES), 1) // GROUP
    out = full[:T]
    for g in range(1, LANES // GROUP):
        out = jnp.where(lane_group == g, full[g * T : (g + 1) * T], out)
    return out


def lanes_of(tile):
    return pl.ds(pl.multiple_of(tile * LANES, LANES), LANES)


def conv_body(lengths, start, left, kv, hyena_q, table, signal, square, flipped):
    span = 2 * T
    turned = lax.broadcasted_iota(jnp.int32, (span, span), 0) + lax.broadcasted_iota(
        jnp.int32, (span, span), 1
    )
    turn = jnp.where(turned == span - 1, 1.0, 0.0).astype(BF16)
    mask = half_masks(lengths, start[0], -T)
    tiles = kv.shape[1] // LANES

    def step(tile, acc):
        at = lanes_of(tile)
        window = jnp.concatenate([left[:, at], kv[:, at]], axis=0)
        out = banded_matmul(table, mask, window, tile)
        signal[:, at] = out
        flipped[:, at] = jnp.dot(turn, window, preferred_element_type=F32).astype(BF16)
        mix = hyena_q[:, at].astype(F32) * out
        return acc + mix * mix

    acc = lax.fori_loop(0, tiles, step, jnp.zeros((T, LANES), F32), unroll=UNROLL)
    square[...] = jnp.broadcast_to(jnp.sum(jnp.transpose(acc), axis=0, keepdims=True), (8, LANES))


def inv_rms_row(squares):
    total = squares[0][0:1, :]
    for s in squares[1:]:
        total = total + s[0:1, :]
    return lax.rsqrt(total / D + 1e-06)


def values_body(signal, hyena_q, gain, s0, s1, s2, s3, values):
    inv = column(inv_rms_row((s0, s1, s2, s3)))

    def step(tile, _):
        at = lanes_of(tile)
        mix = hyena_q[:, at].astype(F32) * signal[:, at]
        values[:, at] = (mix * inv * gain[:, at]).astype(BF16)
        return 0

    lax.fori_loop(0, signal.shape[1] // LANES, step, 0, unroll=UNROLL)


def scores_body(lengths, start, q, k0, k1, k2, og, prob, own, lse):
    span = 3 * T
    query_pos = start[0] + lax.broadcasted_iota(jnp.int32, (span, T), 1)
    key_pos = start[0] - 2 * T + lax.broadcasted_iota(jnp.int32, (span, T), 0)
    allowed = (
        (key_pos >= 0)
        & (key_pos <= query_pos)
        & (query_pos - key_pos <= 2 * T)
        & (doc_of(lengths, key_pos) == doc_of(lengths, query_pos))
    )
    scale = HEAD**-0.5

    def step(h, _):
        at = lanes_of(h)
        keys = jnp.concatenate([k2[:, at], k1[:, at], k0[:, at]], axis=0)
        s = lax.dot_general(keys, q[:, at], (((1,), (1,)), ((), ())), preferred_element_type=F32)
        s = jnp.where(allowed, s * scale, -1e30)
        top = jnp.max(s, axis=0, keepdims=True)
        e = jnp.exp(s - top)
        total = jnp.sum(e, axis=0, keepdims=True)
        p = e * (1.0 / total)
        prob[h] = p
        lse[pl.ds(h, 1), :] = top + jnp.log(total)
        own[:, at] = jnp.dot(p[2 * T :].astype(BF16), og[:, at], preferred_element_type=F32)
        return 0

    lax.fori_loop(0, q.shape[1] // HEAD, step, 0, unroll=2 * UNROLL)


def later_body(
    lengths, start, k0, q1, q2, og1, og2, lse1, lse2, own, signal, hyena_q, gain, prob, grad_values, inner
):
    span = 2 * T
    query_pos = start[0] + T + lax.broadcasted_iota(jnp.int32, (T, span), 1)
    key_pos = start[0] + lax.broadcasted_iota(jnp.int32, (T, span), 0)
    allowed = (query_pos - key_pos <= 2 * T) & (
        doc_of(lengths, key_pos) == doc_of(lengths, query_pos)
    )
    scale = HEAD**-0.5

    def step(h, acc):
        at = lanes_of(h)
        queries = jnp.concatenate([q1[:, at], q2[:, at]], axis=0)
        grads = jnp.concatenate([og1[:, at], og2[:, at]], axis=0)
        row = jnp.concatenate([lse1[pl.ds(h, 1), :], lse2[pl.ds(h, 1), :]], axis=1)
        s = lax.dot_general(k0[:, at], queries, (((1,), (1,)), ((), ())), preferred_element_type=F32)
        p = jnp.exp(jnp.where(allowed, s * scale - row, -1e30))
        prob[h] = p
        gv = own[:, at] + jnp.dot(p.astype(BF16), grads, preferred_element_type=F32)
        gv = gv * gain[:, at]
        grad_values[:, at] = gv
        return acc + gv * (hyena_q[:, at].astype(F32) * signal[:, at])

    acc = lax.fori_loop(0, own.shape[1] // HEAD, step, jnp.zeros((T, LANES), F32), unroll=2 * UNROLL)
    inner[...] = jnp.broadcast_to(jnp.sum(jnp.transpose(acc), axis=0, keepdims=True), (8, LANES))


def signal_grad_body(
    grad_values, signal, hyena_q, s0, s1, s2, s3, i0, i1, i2, i3, grad_hyena_q, grad_signal
):
    inv_row = inv_rms_row((s0, s1, s2, s3))
    inner = i0[0:1, :] + i1[0:1, :] + i2[0:1, :] + i3[0:1, :]
    inv = column(inv_row)
    drop = column(inner * inv_row * inv_row / D)

    def step(tile, _):
        at = lanes_of(tile)
        sig = signal[:, at]
        hq = hyena_q[:, at].astype(F32)
        grad_mix = inv * (grad_values[:, at] - hq * sig * drop)
        grad_hyena_q[:, at] = (grad_mix * sig).astype(BF16)
        grad_signal[:, at] = (grad_mix * hq).astype(BF16)
        return 0

    lax.fori_loop(0, signal.shape[1] // LANES, step, 0, unroll=UNROLL)


def filter_body(lengths, start, flipped, grad_signal, out):
    t = lax.broadcasted_iota(jnp.int32, (T, T), 0)
    l = lax.broadcasted_iota(jnp.int32, (T, T), 1)
    own = l >= T - 1 - t
    mask = same_doc(lengths, start[0], start[0] - 1 - l + jnp.where(own, T, 0))
    lane_group = lax.broadcasted_iota(jnp.int32, (T, LANES), 1) // GROUP
    count = LANES // GROUP

    def step(tile, _):
        at = lanes_of(tile)
        gs = grad_signal[:, at].astype(F32)
        stacked = jnp.concatenate(
            [jnp.where(lane_group == g, gs, 0.0).astype(BF16) for g in range(count)], axis=0
        )
        full = lax.dot_general(
            stacked, flipped[:, at], (((1,), (1,)), ((), ())), preferred_element_type=F32
        )
        rows = []
        for g in range(count):
            corr = full[g * T : (g + 1) * T]
            corr = jnp.where(mask, jnp.where(own, corr[:, :T], corr[:, T:]), 0.0)
            aligned = pltpu.roll(corr, 1, 1, stride=1, stride_axis=0)
            rows.append(jnp.sum(aligned, axis=0, keepdims=True))
        out[pl.ds(pl.multiple_of(tile * 8, 8), 8), :] = jnp.concatenate(rows, axis=0)
        return 0

    lax.fori_loop(0, grad_signal.shape[1] // LANES, step, 0, unroll=2 * UNROLL)


def conv_back_body(lengths, start, grad_signal, right, hyena_k, hyena_v, table, grad_k, grad_v):
    mask = half_masks(lengths, start[0], 0)

    def step(tile, _):
        at = lanes_of(tile)
        window = jnp.concatenate([grad_signal[:, at], right[:, at]], axis=0)
        grad_kv = banded_matmul(table, mask, window, tile)
        grad_k[:, at] = (grad_kv * hyena_v[:, at].astype(F32)).astype(BF16)
        grad_v[:, at] = (grad_kv * hyena_k[:, at].astype(F32)).astype(BF16)
        return 0

    lax.fori_loop(0, hyena_k.shape[1] // LANES, step, 0, unroll=2 * UNROLL)


def delta_body(prob, q, v0, v1, v2, og, own, delta_rows):
    scale = HEAD**-0.5

    def step(h, _):
        at = lanes_of(h)
        vals = jnp.concatenate([v2[:, at], v1[:, at], v0[:, at]], axis=0)
        p = prob[h]
        gp = lax.dot_general(vals, og[:, at], (((1,), (1,)), ((), ())), preferred_element_type=F32)
        delta = jnp.sum(p * gp, axis=0, keepdims=True)
        delta_rows[pl.ds(h, 1), :] = delta
        gs = (p[2 * T :] * (gp[2 * T :] - delta) * scale).astype(BF16)
        own[:, at] = jnp.dot(gs, q[:, at], preferred_element_type=F32)
        return 0

    lax.fori_loop(0, q.shape[1] // HEAD, step, 0, unroll=2 * UNROLL)


def out_body(prob, k0, k1, k2, v0, v1, v2, og, delta_rows, attn_out, grad_q):
    scale = HEAD**-0.5
    over_keys = (((0,), (0,)), ((), ()))

    def step(h, _):
        at = lanes_of(h)
        keys = jnp.concatenate([k2[:, at], k1[:, at], k0[:, at]], axis=0)
        vals = jnp.concatenate([v2[:, at], v1[:, at], v0[:, at]], axis=0)
        p = prob[h]
        gp = lax.dot_general(vals, og[:, at], (((1,), (1,)), ((), ())), preferred_element_type=F32)
        gs = (p * (gp - delta_rows[pl.ds(h, 1), :]) * scale).astype(BF16)
        attn_out[:, at] = lax.dot_general(
            p.astype(BF16), vals, over_keys, preferred_element_type=F32
        ).astype(BF16)
        grad_q[:, at] = lax.dot_general(
            gs, keys, over_keys, preferred_element_type=F32
        ).astype(BF16)
        return 0

    lax.fori_loop(0, k0.shape[1] // HEAD, step, 0, unroll=2 * UNROLL)


def keys_body(prob, v0, q1, q2, og1, og2, delta1, delta2, own, grad_k):
    scale = HEAD**-0.5

    def step(h, _):
        at = lanes_of(h)
        queries = jnp.concatenate([q1[:, at], q2[:, at]], axis=0)
        grads = jnp.concatenate([og1[:, at], og2[:, at]], axis=0)
        delta = jnp.concatenate([delta1[pl.ds(h, 1), :], delta2[pl.ds(h, 1), :]], axis=1)
        gp = lax.dot_general(v0[:, at], grads, (((1,), (1,)), ((), ())), preferred_element_type=F32)
        gs = (prob[h] * (gp - delta) * scale).astype(BF16)
        part = jnp.dot(gs, queries, preferred_element_type=F32)
        grad_k[:, at] = (own[:, at] + part).astype(BF16)
        return 0

    lax.fori_loop(0, v0.shape[1] // HEAD, step, 0, unroll=UNROLL)


def over_sequence(x):
    def send(x, f):
        return lax.ppermute(x, "context", [(i, f(i // 8, i % 8)) for i in range(32)])

    x = x + lax.ppermute(x, "mirror", [(0, 1), (1, 0)])
    parts = [send(x, lambda a, b, d=d: ((a + d) % 4) * 8 + b) for d in (2, 1, 3)]
    x = x + parts[0] + parts[1] + parts[2]
    x = x + send(x, lambda a, b: a * 8 + (b ^ 4))
    parts = [send(x, lambda a, b, d=d: a * 8 + (b ^ d)) for d in (3, 2, 1)]
    return x + parts[0] + parts[1] + parts[2]


def body(hyena_q, hyena_k, hyena_v, filters, norm_gain, attn_q, attn_k, out_grad, doc_lengths):
    rows, channels = hyena_q.shape
    heads = channels // HEAD
    big = (rows, channels)
    band_flops = 2 * (channels // GROUP) * T * 2 * T * LANES
    attn_flops = 2 * heads * 3 * T * T * HEAD
    start = (lax.axis_index(SEQ_AXES) * rows).astype(jnp.int32).reshape(1)
    at = (doc_lengths, start)
    gain = norm_gain[None, :]
    wide = sds(*big)
    half = sds(*big, dtype=BF16)
    small = sds(8, LANES)

    kv = (hyena_k.astype(F32) * hyena_v.astype(F32)).astype(BF16)
    left = shifted(kv, 1)
    og2 = shifted(out_grad, -2)
    q2 = shifted(attn_q, -2)
    og1 = shifted(out_grad, -1)
    q1 = shifted(attn_q, -1)
    k2 = shifted(attn_k, 2)
    k1 = shifted(attn_k, 1)
    groups = filters.shape[0]
    taps = filters.astype(F32)
    fwd_taps = jnp.concatenate([taps[:, :1], taps[:, :0:-1]], axis=1)
    signal, square, flipped = call(
        conv_body,
        (*at, left, kv, hyena_q, fwd_taps),
        (wide, small, sds(2 * rows, channels, dtype=BF16)),
        band_flops,
        8,
    )
    squares = across(square)
    stat = sds(heads, T)
    prob, value_own, lse = call(
        scores_body,
        (*at, attn_q, attn_k, k1, k2, out_grad),
        (sds(heads, 3 * T, T), wide, stat),
        4 * attn_flops // 3,
        16,
        exps=heads * 3 * T * T,
    )
    lse2 = shifted(lse, -2)
    lse1 = shifted(lse, -1)
    (values,) = call(
        values_body, (signal, hyena_q, gain, *squares), (half,), 4 * rows * channels, 8
    )
    v2 = shifted(values, 2)
    v1 = shifted(values, 1)
    prob_later, gain_grad, inner = call(
        later_body,
        (*at, attn_k, q1, q2, og1, og2, lse1, lse2, value_own, signal, hyena_q, gain),
        (sds(heads, T, 2 * T), wide, small),
        4 * attn_flops // 3,
        14,
        exps=heads * 2 * T * T,
    )
    inners = across(inner)
    key_own, delta = call(
        delta_body, (prob, attn_q, values, v1, v2, out_grad), (wide, stat), 4 * attn_flops // 3, 12
    )
    delta2 = shifted(delta, -2)
    delta1 = shifted(delta, -1)
    grad_hyena_q, grad_signal = call(
        signal_grad_body,
        (gain_grad, signal, hyena_q, *squares, *inners),
        (half, half),
        8 * rows * channels,
        10,
    )
    right = shifted(grad_signal, -1)
    (local,) = call(filter_body, (*at, flipped, grad_signal), (sds(groups, LANES),), band_flops, 10)
    grad_filters = over_sequence(local)
    (grad_attn_k,) = call(
        keys_body,
        (prob_later, values, q1, q2, og1, og2, delta1, delta2, key_own),
        (half,),
        4 * attn_flops // 3,
        12,
    )
    grad_hyena_k, grad_hyena_v = call(
        conv_back_body,
        (*at, grad_signal, right, hyena_k, hyena_v, taps),
        (half, half),
        band_flops,
        10,
    )
    attn_out, grad_attn_q = call(
        out_body,
        (prob, attn_k, k1, k2, values, v1, v2, out_grad, delta),
        (half, half),
        3 * attn_flops,
        14,
    )
    return (
        attn_out,
        grad_attn_q,
        grad_attn_k,
        grad_hyena_q,
        grad_hyena_k,
        grad_hyena_v,
        grad_filters,
    )


def solution(mesh):
    tokens = P(SEQ_AXES, "tensor")

    return jax.shard_map(
        body,
        mesh=mesh,
        in_specs=(
            tokens,
            tokens,
            tokens,
            P("tensor", None),
            P("tensor"),
            tokens,
            tokens,
            tokens,
            P(),
        ),
        out_specs=(tokens, tokens, tokens, tokens, tokens, tokens, P("tensor", None)),
        check_vma=False,
    )
```
